128 devices in a mesh: rep: 8 (over z_lo, x), tp: 16 (over y, z_hi, core).
Axes of the slice: x: 4, y: 4, z: 4 (z_hi: 2, z_lo: 2; z = z_hi * 2 + z_lo), core: 2. Of those that a mesh axis runs over, the one named last changes fastest.
Arguments:
- batch_rows: bfloat16 [12288, 4096], P(('rep', 'tp')), may hold values from -6 to 6
- token_slots: int32 [8, 384], P('rep'), may hold values from 0 to 1535, as said below
- holder_map: int32 [8, 16], P('rep'), may hold values from -2 to 111, as said below
- copies: bfloat16 [32768, 16384], P('rep', 'tp'), may hold values from -6 to 6
- upstream: bfloat16 [3072, 16384], P('rep', 'tp'), may hold values from -18 to 18
- up_act: bfloat16 [3072, 16384], P('rep', 'tp'), may hold values from -6 to 6
- master: float32 [4096, 14336], P('rep', 'tp'), may hold values from -0.078125 to 0.078125
- moment1: bfloat16 [4096, 14336], P('rep', 'tp'), may hold values from -0.75 to 0.75
- moment2: bfloat16 [4096, 14336], P('rep', 'tp'), may hold values from 0.049804688 to 2
Outputs:
- master_next: float32 [4096, 14336], P('rep', 'tp')
- moment1_next: bfloat16 [4096, 14336], P('rep', 'tp')
- moment2_next: bfloat16 [4096, 14336], P('rep', 'tp')
- copy_next: bfloat16 [32768, 16384], P('rep', 'tp')
The draws below stay inside these ranges and needn't reach their ends.
Inputs may be any that keep to these rules, and one draw needn't show every extreme that they name: `token_slots`: row r lists 384 distinct rows of replica r's batch. `holder_map`: each row is one replica. A row is either -1 everywhere, or holds -2 at exactly 2 devices and at every other device a distinct piece 7 * j + s (0 <= s < 7) with j one of that row's -2 devices, each such piece exactly once. 4 rows are of the second kind. Columns of copies, upstream and up_act that the steps do not name are not read.
All inputs are finite; a program needn't handle non-finite values.
Results may differ from the reference program's by a relative error of at most 0.02.
Values may be sent and summed in bfloat16 or wider, within the bound.
A program may use at most 128 MiB of HBM per device.

```python
import math
import jax
import jax.numpy as jnp

D = 4096
FF = 14336
TOK = 384
BUF = 1536
WIDE_COLS = 896
UNIT = 128
NARROW_COLS = 1024
N_REP = 8
N_TP = 16


def draw_token_slots(key, part):
    keys = jax.random.split(jax.random.fold_in(key, 11), N_REP)

    def one_replica(sub_key):
        return jax.random.permutation(sub_key, BUF)[:TOK]
    return jax.vmap(one_replica)(keys).astype(jnp.int32)


def draw_holder_map(key, part):
    base = jax.random.fold_in(key, 23)
    order_key, device_key = jax.random.split(base)
    order = jax.random.permutation(order_key, N_REP)
    narrow_flag = jnp.zeros((N_REP,), jnp.int32).at[order[:N_REP // 2]].set(1)
    forced_flag = jnp.arange(N_REP, dtype=jnp.int32) == order[0]
    keys = jax.random.split(device_key, N_REP)
    failed_count = N_TP // 8
    indices = jnp.arange(7 * failed_count, dtype=jnp.int32)
    last_device = N_TP - 1

    def one_replica(sub_key, forced):
        shuffled = jax.random.permutation(sub_key, N_TP).astype(jnp.int32)
        where_last = jnp.argmax(shuffled == last_device).astype(jnp.int32)
        leading = shuffled[0]
        swapped = shuffled.at[where_last].set(leading).at[0].set(last_device)
        shuffled = jnp.where(forced, swapped, shuffled)
        filled = jnp.full((N_TP,), -1, jnp.int32)
        filled = filled.at[shuffled[:failed_count]].set(-2)
        adopted = 7 * shuffled[indices // 7] + indices % 7
        return filled.at[shuffled[failed_count:]].set(adopted)
    maps = jax.vmap(one_replica)(keys, forced_flag)
    return jnp.where(narrow_flag[:, None] == 1, maps, jnp.full_like(maps, -1)).astype(jnp.int32)


def level_of(rng, extent, cuts, low, top_value):
    loudness, own = 1.0, jax.random.fold_in(rng, 6)
    for axis_at, shards_of in cuts:
        draws = jnp.exp(jax.random.uniform(jax.random.fold_in(own, axis_at), (shards_of,), jnp.float32, low / len(cuts), top_value / len(cuts)))
        loudness = loudness * jnp.repeat(draws, extent[axis_at] // shards_of).reshape([-1 if axis == axis_at else 1 for axis in range(len(extent))])
    return loudness


def normal_values(stream_key, extent, deviation, reach, shards=(), kind=jnp.bfloat16):
    loudness = level_of(stream_key, extent, shards, -0.22, 0.18) if shards else 1.0
    result = jax.random.normal(stream_key, extent, jnp.float32) * deviation * loudness
    return jnp.minimum(jnp.maximum(result, -reach), reach).astype(kind)


def setup_inputs(seed: int = 0) -> dict:
    key_of = jax.random.split(jax.random.key(seed), 10)
    return {
        "batch_rows": normal_values(key_of[0], (N_REP * BUF, D), 1.0, 6.0, ((0, 128),)),
        "token_slots": draw_token_slots(jax.random.fold_in(key_of[9], 71), 0),
        "holder_map": draw_holder_map(jax.random.fold_in(key_of[9], 71), 0),
        "copies": normal_values(key_of[3], (N_REP * D, N_TP * NARROW_COLS), 1.0, 6.0, ((0, 8), (1, 16))),
        "upstream": normal_values(key_of[4], (N_REP * TOK, N_TP * NARROW_COLS), 3.0, 18.0, ((0, 8), (1, 16))),
        "up_act": normal_values(key_of[5], (N_REP * TOK, N_TP * NARROW_COLS), 1.0, 6.0, ((0, 8), (1, 16))),
        "master": normal_values(key_of[6], (D, FF), 0.005, 0.078125, ((0, 8), (1, 16)), jnp.float32),
        "moment1": normal_values(key_of[7], (D, FF), 0.05, 0.75, ((0, 8), (1, 16))),
        "moment2": jnp.clip(jnp.exp(math.log(2.0) - 3.6927934 * jax.random.uniform(key_of[8], (D, FF), jnp.float32) ** level_of(key_of[8], (D, FF), ((0, 8), (1, 16)), -0.2, 0.2)), 0.049804688, 2.0).astype(jnp.bfloat16),
    }


beta_one = 0.9
beta_two = 0.95
bias_one = 1.0 - 0.9 ** 10
bias_two = 1.0 - 0.95 ** 10
learn_rate = 0.05
weight_decay = 0.1
epsilon = 1e-08

def assemble(layout, holders):
    height = layout.shape[0]
    pieces = layout.reshape(height, N_TP, NARROW_COLS)
    own_block = pieces[:, :, :WIDE_COLS]
    adopted_part = pieces[:, :, WIDE_COLS:]
    targets = jnp.arange(7 * N_TP, dtype=jnp.int32)
    owners = jnp.argmax(holders[None, :] == targets[:, None], axis=1).astype(jnp.int32)
    adopted = jnp.take(adopted_part, owners, axis=1).reshape(height, N_TP, WIDE_COLS)
    failed = holders == -2
    blocks = jnp.where(failed[None, :, None], adopted, own_block)
    return blocks.reshape(height, FF)

def reference(batch_rows, token_slots, holder_map, copies, upstream, up_act, master, moment1, moment2):
    scaling = 1.0 / math.sqrt(D)
    gradient = jnp.zeros((D, FF), jnp.float32)
    for replica in range(N_REP):
        batch_part = batch_rows[replica * BUF:(replica + 1) * BUF]
        inputs = jnp.take(batch_part, token_slots[replica].astype(jnp.int32), axis=0)
        holders = holder_map[replica].astype(jnp.int32)
        weight = assemble(copies[replica * D:(replica + 1) * D], holders)
        cotangent = assemble(upstream[replica * TOK:(replica + 1) * TOK], holders)
        opened = assemble(up_act[replica * TOK:(replica + 1) * TOK], holders)
        gate_pre = jnp.dot(inputs, weight, preferred_element_type=jnp.float32) * scaling
        logistic = jax.nn.sigmoid(gate_pre)
        gate_grad = (cotangent.astype(jnp.float32) * opened.astype(jnp.float32) * logistic * (1.0 + gate_pre * (1.0 - logistic))).astype(jnp.bfloat16)
        partial_value = jnp.dot(inputs.T, gate_grad, preferred_element_type=jnp.float32) * scaling
        gradient = gradient + partial_value.astype(jnp.bfloat16).astype(jnp.float32)
    first_new = beta_one * moment1.astype(jnp.float32) + (1.0 - beta_one) * gradient
    second_new = beta_two * moment2.astype(jnp.float32) + (1.0 - beta_two) * gradient * gradient
    step_size = first_new / bias_one / (jnp.sqrt(second_new / bias_two) + epsilon)
    master_next = master - learn_rate * (step_size + weight_decay * master)
    fresh_copy = master_next.astype(jnp.bfloat16)
    blocks = fresh_copy.reshape(D, N_TP, WIDE_COLS)
    unit_view = fresh_copy.reshape(D, 7 * N_TP, UNIT)
    outputs = []
    for replica in range(N_REP):
        holders = holder_map[replica].astype(jnp.int32)
        picked = jnp.take(unit_view, jnp.maximum(holders, 0), axis=1)
        picked = jnp.where((holders >= 0)[None, :, None], picked, jnp.zeros_like(picked))
        joined = jnp.concatenate([blocks, picked], axis=2)
        joined = jnp.where((holders == -2)[None, :, None], jnp.zeros_like(joined), joined)
        outputs.append(joined.reshape(D, N_TP * NARROW_COLS))
    copy_next = jnp.concatenate(outputs, axis=0)
    return (master_next, first_new.astype(jnp.bfloat16), second_new.astype(jnp.bfloat16), copy_next)
```

```python
import math

import jax
import jax.numpy as jnp
from jax import lax
from jax.sharding import PartitionSpec as P

beta_one = 0.9
beta_two = 0.95
bias_one = 1.0 - 0.9**10
bias_two = 1.0 - 0.95**10
learn_rate = 0.05
weight_decay = 0.1
epsilon = 1e-08


def picked(indices, table):
    one_hot = (indices[:, None] == jnp.arange(table.shape[0], dtype=jnp.int32)[None, :]).astype(jnp.bfloat16)
    return jnp.dot(one_hot, table, preferred_element_type=jnp.float32).astype(jnp.bfloat16)


def on_device(
    batch_rows, token_slots, holder_map, copies, upstream, up_act, master, moment1, moment2
):
    tp_count = lax.axis_size("tp")
    rep_count = lax.axis_size("rep")
    position = lax.axis_index("tp")
    holders = holder_map[0]
    own_entry = jnp.sum(jnp.where(jnp.arange(tp_count) == position, holders, 0))
    all_holders = lax.all_gather(holders, "rep")
    unit_cols = copies.shape[1] // 8
    wide_cols = 7 * unit_cols
    scaling = 1.0 / math.sqrt(copies.shape[0])

    columns = lax.all_to_all(batch_rows, "tp", split_axis=1, concat_axis=0, tiled=True)
    chosen = picked(token_slots[0], columns)
    inputs = lax.all_gather(chosen, "tp", axis=1, tiled=True)
    gate_pre = jnp.dot(inputs, copies, preferred_element_type=jnp.float32) * scaling
    logistic = jax.nn.sigmoid(gate_pre)
    gate_grad = (
        upstream.astype(jnp.float32)
        * up_act.astype(jnp.float32)
        * logistic
        * (1.0 + gate_pre * (1.0 - logistic))
    ).astype(jnp.bfloat16)
    tokens = gate_grad.shape[0]
    pooled = lax.all_to_all(
        jnp.broadcast_to(gate_grad[:, wide_cols:], (tp_count, tokens, unit_cols)),
        "tp", split_axis=0, concat_axis=0, tiled=True,
    )
    wanted = position * 7 + jnp.arange(7, dtype=jnp.int32)
    choice = (holders[None, :] == wanted[:, None]).astype(jnp.bfloat16)
    rebuilt = jnp.concatenate(
        [
            jnp.sum(jnp.where(choice[s, :, None, None] > 0, pooled, jnp.zeros_like(pooled)), axis=0)
            for s in range(7)
        ],
        axis=1,
    )
    block_grad = jnp.where(own_entry == -2, rebuilt, gate_grad[:, :wide_cols])
    product = lax.dot_general(
        inputs, block_grad, (((0,), (0,)), ((), ())), preferred_element_type=jnp.float32
    )
    gradient = lax.psum_scatter(
        (product * scaling).astype(jnp.bfloat16), "rep", scatter_dimension=0, tiled=True
    ).astype(jnp.float32)
    first_new = beta_one * moment1.astype(jnp.float32) + (1.0 - beta_one) * gradient
    second_new = beta_two * moment2.astype(jnp.float32) + (1.0 - beta_two) * gradient * gradient
    step_size = first_new / bias_one / (jnp.sqrt(second_new / bias_two) + epsilon)
    master_next = master - learn_rate * (step_size + weight_decay * master)
    fresh = master_next.astype(jnp.bfloat16)
    full_block = lax.all_gather(fresh, "rep", axis=0, tiled=True)

    own_rows = fresh.shape[0]
    strip = own_rows // tp_count
    spread = lax.all_to_all(fresh, "tp", split_axis=0, concat_axis=0, tiled=True)
    table = spread.reshape(tp_count, strip, 7, unit_cols).transpose(0, 2, 1, 3)
    routed = picked(all_holders.reshape(-1), table.reshape(tp_count * 7, strip * unit_cols))
    routed = routed.reshape(rep_count, tp_count, strip, unit_cols)
    routed = lax.all_to_all(routed, "tp", split_axis=1, concat_axis=2, tiled=True)
    routed = routed.reshape(rep_count * own_rows, unit_cols)
    adopted = lax.all_to_all(routed, "rep", split_axis=0, concat_axis=0, tiled=True)
    copy_next = jnp.concatenate([full_block, adopted], axis=1)
    copy_next = jnp.where(own_entry == -2, jnp.zeros_like(copy_next), copy_next)
    return (master_next, first_new.astype(jnp.bfloat16), second_new.astype(jnp.bfloat16), copy_next)


def solution(mesh):
    placed = (
        P(("rep", "tp"), None),
        P("rep", None),
        P("rep", None),
        P("rep", "tp"),
        P("rep", "tp"),
        P("rep", "tp"),
        P("rep", "tp"),
        P("rep", "tp"),
        P("rep", "tp"),
    )
    return jax.shard_map(
        on_device,
        mesh=mesh,
        in_specs=placed,
        out_specs=(P("rep", "tp"), P("rep", "tp"), P("rep", "tp"), P("rep", "tp")),
        check_vma=False,
    )
```

```python
import functools
import math

import jax
import jax.numpy as jnp
from jax import lax
from jax.experimental import pallas as pl
from jax.experimental.pallas import tpu as pltpu
from jax.sharding import PartitionSpec as P

beta_one = 0.9
beta_two = 0.95
bias_one = 1.0 - 0.9**10
bias_two = 1.0 - 0.95**10
learn_rate = 0.05
weight_decay = 0.1
epsilon = 1e-08

D, TOK, WIDE, UNIT, NARROW = 4096, 384, 896, 128, 1024
REP, TP = 8, 16
OWN, SHARE = 96, 256
ROWS = D // REP
STRIP = ROWS // TP
SEVEN = WIDE // UNIT
PART = TOK // (TP // 2)
SCALING = 1.0 / math.sqrt(D)
MESH = pl.DeviceIdType.MESH
F32, BF16 = jnp.float32, jnp.bfloat16


class Place:
    def __init__(self):
        r, t = lax.axis_index("rep"), lax.axis_index("tp")
        self.r, self.t = r, t
        x, zl = r % 4, r // 4
        y, zh, c = t // 4, (t // 2) % 2, t % 2
        self.core = c
        self.chip = t // 2
        self.sibling = (r, t + 1 - 2 * c)

        def rep_id(step, flip):
            return (x + step) % 4 + 4 * ((zl + flip) % 2)

        def tp_id(step, flip):
            return ((y + step) % 4) * 4 + ((zh + flip) % 2) * 2 + c

        self.rep_ids = [[rep_id(s, f) for s in (0, 1, 3, 2)] for f in (0, 1)]
        self.tp_ids = [[tp_id(s, f) for s in (0, 1, 3, 2)] for f in (0, 1)]

    def rep_dev(self, other):
        return (other, self.t)

    def tp_dev(self, other):
        return (self.r, other)


def greet(place):
    barrier = pltpu.get_barrier_semaphore()

    def rep_mate(k, carry):
        pl.semaphore_signal(barrier, inc=1, device_id=((place.r + k) % REP, place.t), device_id_type=MESH)
        return carry

    def tp_mate(k, carry):
        pl.semaphore_signal(barrier, inc=1, device_id=(place.r, (place.t + k) % TP), device_id_type=MESH)
        return carry

    lax.fori_loop(1, REP, rep_mate, 0)
    lax.fori_loop(1, TP, tp_mate, 0)
    pl.semaphore_wait(barrier, REP + TP - 2)


class Tree:
    def __init__(self, view, ids, dev, ssem, rsem, extent, first):
        (me, nx, pv, op), (me_p, nx_p, pv_p, op_p) = ids
        to_nx, to_pv, to_pair = dev(nx), dev(pv), dev(me_p)
        half, a_half, rest = extent // 2, first // 2, extent - first
        self.rest, self.names = rest, dict(me=me, nx=nx, pv=pv, op=op, me_p=me_p, nx_p=nx_p, pv_p=pv_p, op_p=op_p)
        sent = {
            1: (me, 0, extent, to_nx), 2: (me, 0, extent, to_pv), 3: (me, 0, first, to_pair), 4: (me, first, rest, to_pair),
            5: (me_p, 0, first, to_nx), 6: (me_p, 0, first, to_pv), 7: (pv, 0, half, to_nx), 8: (nx, half, half, to_pv),
            9: (pv_p, 0, a_half, to_nx), 10: (nx_p, a_half, a_half, to_pv),
            11: (pv, first, rest, to_pair), 12: (nx, first, rest, to_pair), 13: (op, first, rest, to_pair),
        }
        got = {1: pv, 2: nx, 3: me_p, 4: me_p, 5: pv_p, 6: nx_p, 7: op, 8: op, 9: op_p, 10: op_p, 11: pv_p, 12: nx_p, 13: op_p}
        skipped = () if rest else (4, 11, 12, 13)
        self.out, self.into = {}, {}
        for i, (chunk, low, count, to) in sent.items():
            if i not in skipped:
                for book, which in ((self.out, chunk), (self.into, got[i])):
                    ref = view(which, low, count)
                    book[i] = pltpu.make_async_remote_copy(
                        src_ref=ref, dst_ref=ref, send_sem=ssem.at[i - 1], recv_sem=rsem.at[i - 1],
                        device_id=to, device_id_type=MESH,
                    )

    def start(self, *which):
        for i in which:
            if i in self.out:
                self.out[i].start()

    def wait(self, *which):
        for i in which:
            if i in self.into:
                self.into[i].wait_recv()

    def steps(self, done):
        def pair():
            self.wait(3)
            self.start(5, 6)
            if not self.rest:
                done("me_p")

        def previous():
            self.wait(1)
            self.start(7, 11)
            done("pv")

        def following():
            self.wait(2)
            self.start(8, 12)
            done("nx")

        def pair_previous():
            self.wait(5)
            self.start(9)
            if not self.rest:
                done("pv_p")

        def pair_following():
            self.wait(6)
            self.start(10)
            if not self.rest:
                done("nx_p")

        def opposite():
            self.wait(7, 8)
            self.start(13)
            done("op")

        def rests():
            if self.rest:
                self.wait(4)
                done("me_p")
                self.wait(11)
                done("pv_p")
                self.wait(12)
                done("nx_p")

        def last():
            self.wait(9, 10, 13)
            done("op_p")

        return [pair, previous, following, pair_previous, pair_following, opposite, rests, last]

    def begin(self):
        self.start(3, 1, 2, 4)

    def drain(self):
        for copy in self.out.values():
            copy.wait_send()


ORDER = ("me", "pv", "nx", "me_p", "op", "pv_p", "nx_p", "op_p")


class Siblings:
    def __init__(self, tree, view, extent, place, ssem, rsem):
        self.out, self.into = {}, {}
        for n, name in enumerate(ORDER):
            mine = tree.names[name]
            for book, which in ((self.out, mine), (self.into, mine + 1 - 2 * place.core)):
                ref = view(which, 0, extent)
                book[name] = pltpu.make_async_remote_copy(
                    src_ref=ref, dst_ref=ref, send_sem=ssem.at[n], recv_sem=rsem.at[n],
                    device_id=place.sibling, device_id_type=MESH,
                )

    def start(self, name):
        self.out[name].start()

    def wait(self, name):
        self.into[name].wait_recv()

    def drain(self):
        for copy in self.out.values():
            copy.wait_send()


def front_kernel(
    rows_ref, slots_ref, holders_ref, map_ref, copies_ref, upstream_ref, act_ref,
    inputs_out, grad_out, holders_out,
    own_rows, spread, inputs, weight, total, grad, pieces,
    map_s, map_r, row_s, row_r, tree_s, tree_r, sib_s, sib_r, tree2_s, tree2_r, sib2_s, sib2_r, local,
):
    place = Place()
    t = place.t
    load_rows = pltpu.make_async_copy(rows_ref, own_rows, local.at[0])
    load_rows.start()
    load_weight = pltpu.make_async_copy(copies_ref, weight, local.at[1])
    load_weight.start()
    greet(place)
    load_rows.wait()

    def share_to(k):
        to = (t + k) % TP
        return pltpu.make_async_remote_copy(
            src_ref=own_rows.at[:, pl.ds(pl.multiple_of(to * SHARE, SHARE), SHARE)],
            dst_ref=spread.at[pl.ds(pl.multiple_of(t * OWN, OWN), OWN), :],
            send_sem=row_s.at[k], recv_sem=row_r.at[k],
            device_id=(place.r, to), device_id_type=MESH,
        )

    def share_from(k):
        source = (t + TP - k) % TP
        ref = spread.at[pl.ds(pl.multiple_of(source * OWN, OWN), OWN), :]
        return pltpu.make_async_remote_copy(
            src_ref=ref, dst_ref=ref, send_sem=row_s.at[k], recv_sem=row_r.at[k],
            device_id=(place.r, source), device_id_type=MESH,
        )

    lax.fori_loop(1, TP, lambda k, c: (share_to(k).start(), c)[1], 0)

    def map_to(k):
        return pltpu.make_async_remote_copy(
            src_ref=map_ref, dst_ref=holders_out.at[place.r], send_sem=map_s.at[k], recv_sem=map_r.at[k],
            device_id=((place.r + k) % REP, t), device_id_type=MESH,
        )

    def map_from(k):
        source = (place.r + REP - k) % REP
        return pltpu.make_async_remote_copy(
            src_ref=map_ref, dst_ref=holders_out.at[source], send_sem=map_s.at[k], recv_sem=map_r.at[k],
            device_id=(source, t), device_id_type=MESH,
        )

    lax.fori_loop(1, REP, lambda k, c: (map_to(k).start(), c)[1], 0)
    own_map = pltpu.make_async_copy(map_ref, holders_out.at[place.r], local.at[5])
    own_map.start()
    own = pltpu.make_async_copy(
        own_rows.at[:, pl.ds(pl.multiple_of(t * SHARE, SHARE), SHARE)],
        spread.at[pl.ds(pl.multiple_of(t * OWN, OWN), OWN), :],
        local.at[2],
    )
    own.start()
    own.wait()
    lax.fori_loop(1, TP, lambda k, c: (share_from(k).wait_recv(), c)[1], 0)

    slots = slots_ref[...]
    found = jnp.zeros((TOK, SHARE), F32)
    block = 512
    for b in range(TP * OWN // block):
        places = lax.broadcasted_iota(jnp.int32, (TOK, block), 1) + b * block
        one_hot = jnp.where(slots == places, 1.0, 0.0).astype(BF16)
        found += jnp.dot(one_hot, spread[b * block : (b + 1) * block, :], preferred_element_type=F32)
    inputs[t] = found.astype(BF16)

    def input_view(chunk, low, count):
        return inputs.at[chunk, pl.ds(low, count), :]

    tree = Tree(input_view, place.tp_ids, place.tp_dev, tree_s, tree_r, TOK, 224)
    sibs = Siblings(tree, input_view, TOK, place, sib_s, sib_r)
    tree.begin()
    sibs.start("me")
    load_weight.wait()

    def multiplied(chunk, first=False):
        depth = pl.ds(pl.multiple_of(chunk * SHARE, SHARE), SHARE)
        for n in range(4):
            cols = slice(n * 256, (n + 1) * 256)
            part = jnp.dot(inputs[chunk], weight[depth, cols], preferred_element_type=F32)
            total[:, cols] = part if first else total[:, cols] + part

    multiplied(t, True)
    waiting = ["me"]

    def whole(name):
        sibs.start(name)
        multiplied(tree.names[name])
        before = waiting.pop()
        sibs.wait(before)
        multiplied(tree.names[before] + 1 - 2 * place.core)
        waiting.append(name)

    for step in tree.steps(whole):
        step()
    sibs.wait(waiting[0])
    multiplied(tree.names[waiting[0]] + 1 - 2 * place.core)

    store_inputs = pltpu.make_async_copy(inputs, inputs_out, local.at[3])
    store_inputs.start()

    def gate_rows(n, carry):
        at = pl.ds(pl.multiple_of(n * 16, 16), 16)
        gate = total[at, :] * SCALING
        logistic = 1.0 / (1.0 + jnp.exp(-gate))
        grad[at, :] = (
            upstream_ref[at, :].astype(F32) * act_ref[at, :].astype(F32) * logistic * (1.0 + gate * (1.0 - logistic))
        ).astype(BF16)
        return carry

    lax.fori_loop(0, TOK // 16, gate_rows, 0)
    pieces[t] = grad[:, WIDE:]

    def piece_view(chunk, low, count):
        return pieces.at[chunk, pl.ds(low, count), :]

    tree2 = Tree(piece_view, place.tp_ids, place.tp_dev, tree2_s, tree2_r, TOK, 224)
    sibs2 = Siblings(tree2, piece_view, TOK, place, sib2_s, sib2_r)
    tree2.begin()
    sibs2.start("me")
    for step in tree2.steps(sibs2.start):
        step()
    for name in ORDER:
        sibs2.wait(name)

    own_entry = holders_ref[0, t]
    for s in range(SEVEN):
        wanted = t * SEVEN + s
        owner = jnp.int32(0)
        for other in range(TP):
            owner = jnp.where(holders_ref[0, other] == wanted, other, owner)
        cols = slice(s * UNIT, (s + 1) * UNIT)
        grad[:, cols] = jnp.where(own_entry == -2, pieces[owner], grad[:, cols])
    store_grad = pltpu.make_async_copy(grad.at[:, pl.ds(0, WIDE)], grad_out, local.at[4])
    store_grad.start()

    lax.fori_loop(1, TP, lambda k, c: (share_to(k).wait_send(), c)[1], 0)
    for book in (tree, sibs, tree2, sibs2):
        book.drain()
    own_map.wait()
    lax.fori_loop(1, REP, lambda k, c: (map_from(k).wait_recv(), c)[1], 0)
    lax.fori_loop(1, REP, lambda k, c: (map_to(k).wait_send(), c)[1], 0)
    store_inputs.wait()
    store_grad.wait()


def back_kernel(
    inputs_ref, grad_ref, holders_ref, master_ref, one_ref, two_ref,
    master_out, one_out, two_out, full_out, adopted_out,
    parts, grads, total, fresh, strips, spread, picked, routed, adopted, master, one, two,
    swap_s, swap_r, part_s, part_r, sib_s, sib_r, grad_s, grad_r, fresh_s, fresh_r,
    p1_s, p1_r, p2_s, p2_r, p3_s, p3_r, local, outs,
):
    place = Place()
    r, t = place.r, place.t
    load_grad = pltpu.make_async_copy(grad_ref, grads.at[r], local.at[0])
    load_grad.start()
    loads = [
        pltpu.make_async_copy(a, b, local.at[n + 1])
        for n, (a, b) in enumerate(((master_ref, master), (one_ref, one), (two_ref, two)))
    ]
    for load in loads:
        load.start()
    greet(place)

    mine_rows = pl.ds(pl.multiple_of(place.chip * PART, PART), PART)
    mine_cols = pl.ds(pl.multiple_of(place.core * SHARE, SHARE), SHARE)

    def swap_to(k):
        to = (r + k) % REP
        return pltpu.make_async_remote_copy(
            src_ref=inputs_ref.at[2 * to + place.core, mine_rows, :],
            dst_ref=parts.at[r, mine_rows, mine_cols],
            send_sem=swap_s.at[k], recv_sem=swap_r.at[k], device_id=(to, t), device_id_type=MESH,
        )

    def swap_from(k):
        source = (r + REP - k) % REP
        ref = parts.at[source, mine_rows, mine_cols]
        return pltpu.make_async_remote_copy(
            src_ref=ref, dst_ref=ref, send_sem=swap_s.at[k], recv_sem=swap_r.at[k],
            device_id=(source, t), device_id_type=MESH,
        )

    lax.fori_loop(1, REP, lambda k, c: (swap_to(k).start(), c)[1], 0)
    own = pltpu.make_async_copy(
        inputs_ref.at[2 * r + place.core, mine_rows, :], parts.at[r, mine_rows, mine_cols], local.at[4]
    )
    own.start()

    def grad_view(chunk, low, count):
        return grads.at[chunk, pl.ds(low, count), :]

    load_grad.wait()
    gtree = Tree(grad_view, place.rep_ids, place.rep_dev, grad_s, grad_r, TOK, 224)
    gtree.begin()

    def part_view(chunk, low, count):
        at, side = chunk // 2, chunk % 2
        return parts.at[
            pl.ds(low, count),
            pl.ds(pl.multiple_of(at * PART, PART), PART),
            pl.ds(pl.multiple_of(side * SHARE, SHARE), SHARE),
        ]

    own.wait()
    lax.fori_loop(1, REP, lambda k, c: (swap_from(k).wait_recv(), c)[1], 0)
    ptree = Tree(part_view, place.tp_ids, place.tp_dev, part_s, part_r, REP, REP)
    sibs = Siblings(ptree, part_view, REP, place, sib_s, sib_r)
    ptree.begin()
    sibs.start("me")

    def multiplied(chunk, first=False):
        part = lax.dot_general(
            parts[chunk], grads[chunk], (((0,), (0,)), ((), ())), preferred_element_type=F32
        )
        total[...] = part if first else total[...] + part

    ready = []
    gsteps = gtree.steps(lambda name: multiplied(gtree.names[name]))
    gsteps[0]()
    for step in ptree.steps(sibs.start):
        step()
    for name in ORDER:
        sibs.wait(name)
    multiplied(r, True)
    for step in gsteps[1:]:
        step()

    for load in loads:
        load.wait()

    def adam_rows(n, carry):
        at = pl.ds(pl.multiple_of(n * 16, 16), 16)
        gradient = total[at, :] * SCALING
        first_new = beta_one * one[at, :].astype(F32) + (1.0 - beta_one) * gradient
        second_new = beta_two * two[at, :].astype(F32) + (1.0 - beta_two) * gradient * gradient
        step_size = first_new / bias_one / (jnp.sqrt(second_new / bias_two) + epsilon)
        old = master[at, :]
        new = old - learn_rate * (step_size + weight_decay * old)
        master[at, :] = new
        one[at, :] = first_new.astype(BF16)
        two[at, :] = second_new.astype(BF16)
        low = new.astype(BF16)
        fresh[r, at, :] = low
        for s in range(SEVEN):
            strips[s, at, :] = low[:, s * UNIT : (s + 1) * UNIT]
        return carry

    lax.fori_loop(0, ROWS // 16, adam_rows, 0)

    def fresh_view(chunk, low, count):
        return fresh.at[chunk, pl.ds(low, count), :]

    ftree = Tree(fresh_view, place.rep_ids, place.rep_dev, fresh_s, fresh_r, ROWS, 384)

    def one_to(k):
        to = (t + k) % TP
        return pltpu.make_async_remote_copy(
            src_ref=strips.at[:, pl.ds(pl.multiple_of(to * STRIP, STRIP), STRIP), :],
            dst_ref=spread.at[pl.ds(t * SEVEN, SEVEN)],
            send_sem=p1_s.at[k], recv_sem=p1_r.at[k], device_id=(r, to), device_id_type=MESH,
        )

    def one_from(k):
        source = (t + TP - k) % TP
        ref = spread.at[pl.ds(source * SEVEN, SEVEN)]
        return pltpu.make_async_remote_copy(
            src_ref=ref, dst_ref=ref, send_sem=p1_s.at[k], recv_sem=p1_r.at[k],
            device_id=(r, source), device_id_type=MESH,
        )

    lax.fori_loop(1, TP, lambda k, c: (one_to(k).start(), c)[1], 0)
    ftree.begin()
    spread[pl.ds(t * SEVEN, SEVEN)] = strips[:, pl.ds(pl.multiple_of(t * STRIP, STRIP), STRIP), :]
    stores = [
        pltpu.make_async_copy(a, b, outs.at[n])
        for n, (a, b) in enumerate(((master, master_out), (one, one_out), (two, two_out), (fresh.at[r], full_out.at[r])))
    ]
    for store in stores:
        store.start()

    lax.fori_loop(1, TP, lambda k, c: (one_from(k).wait_recv(), c)[1], 0)

    def pick(n, carry):
        q, to = n // TP, n % TP
        piece = holders_ref[q, 0, to]
        value = spread[jnp.maximum(piece, 0)]
        picked[to, q] = jnp.where(piece >= 0, value, jnp.zeros_like(value))
        return carry

    lax.fori_loop(0, REP * TP, pick, 0)

    def two_to(k):
        to = (t + k) % TP
        return pltpu.make_async_remote_copy(
            src_ref=picked.at[to], dst_ref=routed.at[:, pl.ds(pl.multiple_of(t * STRIP, STRIP), STRIP), :],
            send_sem=p2_s.at[k], recv_sem=p2_r.at[k], device_id=(r, to), device_id_type=MESH,
        )

    def two_from(k):
        source = (t + TP - k) % TP
        ref = routed.at[:, pl.ds(pl.multiple_of(source * STRIP, STRIP), STRIP), :]
        return pltpu.make_async_remote_copy(
            src_ref=ref, dst_ref=ref, send_sem=p2_s.at[k], recv_sem=p2_r.at[k],
            device_id=(r, source), device_id_type=MESH,
        )

    lax.fori_loop(1, TP, lambda k, c: (two_to(k).start(), c)[1], 0)
    routed[:, pl.ds(pl.multiple_of(t * STRIP, STRIP), STRIP), :] = picked[t]

    def stored(name):
        chunk = ftree.names[name]
        store = pltpu.make_async_copy(fresh.at[chunk], full_out.at[chunk], outs.at[4 + ORDER.index(name)])
        store.start()
        stores.append(store)

    fsteps = ftree.steps(stored)
    for step in fsteps[:3]:
        step()

    lax.fori_loop(1, TP, lambda k, c: (two_from(k).wait_recv(), c)[1], 0)

    def three_to(k):
        to = (r + k) % REP
        return pltpu.make_async_remote_copy(
            src_ref=routed.at[to], dst_ref=adopted.at[r], send_sem=p3_s.at[k], recv_sem=p3_r.at[k],
            device_id=(to, t), device_id_type=MESH,
        )

    def three_from(k):
        source = (r + REP - k) % REP
        return pltpu.make_async_remote_copy(
            src_ref=adopted.at[source], dst_ref=adopted.at[source], send_sem=p3_s.at[k], recv_sem=p3_r.at[k],
            device_id=(source, t), device_id_type=MESH,
        )

    lax.fori_loop(1, REP, lambda k, c: (three_to(k).start(), c)[1], 0)
    adopted[r] = routed[r]
    for step in fsteps[3:]:
        step()
    lax.fori_loop(1, REP, lambda k, c: (three_from(k).wait_recv(), c)[1], 0)
    store = pltpu.make_async_copy(adopted, adopted_out, outs.at[12])
    store.start()
    stores.append(store)

    for book in (ptree, sibs, gtree, ftree):
        book.drain()
    lax.fori_loop(1, REP, lambda k, c: (swap_to(k).wait_send(), c)[1], 0)
    lax.fori_loop(1, TP, lambda k, c: (one_to(k).wait_send(), c)[1], 0)
    lax.fori_loop(1, TP, lambda k, c: (two_to(k).wait_send(), c)[1], 0)
    lax.fori_loop(1, REP, lambda k, c: (three_to(k).wait_send(), c)[1], 0)
    for store in stores:
        store.wait()


ANY = pl.BlockSpec(memory_space=pl.ANY)
VM = pl.BlockSpec(memory_space=pltpu.VMEM)
SM = pl.BlockSpec(memory_space=pltpu.SMEM)


def sems(*counts):
    return [pltpu.SemaphoreType.DMA((n,)) for n in counts for _ in (0, 1)]


def on_device(
    batch_rows, token_slots, holder_map, copies, upstream, up_act, master, moment1, moment2
):
    own_entry = jnp.sum(jnp.where(jnp.arange(TP) == lax.axis_index("tp"), holder_map[0], 0))
    inputs, block_grad, all_holders = pl.pallas_call(
        front_kernel,
        out_shape=(
            jax.ShapeDtypeStruct((TP, TOK, SHARE), BF16),
            jax.ShapeDtypeStruct((TOK, WIDE), BF16),
            jax.ShapeDtypeStruct((REP, 1, TP), jnp.int32),
        ),
        in_specs=[ANY, VM, SM, ANY, ANY, VM, VM],
        out_specs=(ANY, ANY, ANY),
        scratch_shapes=[
            pltpu.VMEM((OWN, D), BF16),
            pltpu.VMEM((TP * OWN, SHARE), BF16),
            pltpu.VMEM((TP, TOK, SHARE), BF16),
            pltpu.VMEM((D, NARROW), BF16),
            pltpu.VMEM((TOK, NARROW), F32),
            pltpu.VMEM((TOK, NARROW), BF16),
            pltpu.VMEM((TP, TOK, UNIT), BF16),
            *sems(REP, TP, 13, 8, 13, 8),
            pltpu.SemaphoreType.DMA((6,)),
        ],
        compiler_params=pltpu.CompilerParams(
            collective_id=0, has_side_effects=True, vmem_limit_bytes=56 << 20
        ),
        name="front",
    )(batch_rows, token_slots.reshape(TOK, 1), holder_map, holder_map, copies, upstream, up_act)
    master_next, one_next, two_next, full, adopted = pl.pallas_call(
        back_kernel,
        out_shape=(
            jax.ShapeDtypeStruct((ROWS, WIDE), F32),
            jax.ShapeDtypeStruct((ROWS, WIDE), BF16),
            jax.ShapeDtypeStruct((ROWS, WIDE), BF16),
            jax.ShapeDtypeStruct((REP, ROWS, WIDE), BF16),
            jax.ShapeDtypeStruct((REP, ROWS, UNIT), BF16),
        ),
        in_specs=[ANY, ANY, SM, ANY, ANY, ANY],
        out_specs=(ANY,) * 5,
        scratch_shapes=[
            pltpu.VMEM((REP, TOK, ROWS), BF16),
            pltpu.VMEM((REP, TOK, WIDE), BF16),
            pltpu.VMEM((ROWS, WIDE), F32),
            pltpu.VMEM((REP, ROWS, WIDE), BF16),
            pltpu.VMEM((SEVEN, ROWS, UNIT), BF16),
            pltpu.VMEM((TP * SEVEN, STRIP, UNIT), BF16),
            pltpu.VMEM((TP, REP, STRIP, UNIT), BF16),
            pltpu.VMEM((REP, ROWS, UNIT), BF16),
            pltpu.VMEM((REP, ROWS, UNIT), BF16),
            pltpu.VMEM((ROWS, WIDE), F32),
            pltpu.VMEM((ROWS, WIDE), BF16),
            pltpu.VMEM((ROWS, WIDE), BF16),
            *sems(REP, 13, 8, 13, 13, TP, TP, REP),
            pltpu.SemaphoreType.DMA((5,)),
            pltpu.SemaphoreType.DMA((13,)),
        ],
        compiler_params=pltpu.CompilerParams(
            collective_id=1, has_side_effects=True, vmem_limit_bytes=56 << 20
        ),
        name="back",
    )(inputs, block_grad, all_holders, master, moment1, moment2)
    copy_next = jnp.concatenate([full.reshape(D, WIDE), adopted.reshape(D, UNIT)], axis=1)
    copy_next = jnp.where(own_entry == -2, jnp.zeros_like(copy_next), copy_next)
    return master_next, one_next, two_next, copy_next


def solution(mesh):
    placed = (
        P(("rep", "tp"), None),
        P("rep", None),
        P("rep", None),
        P("rep", "tp"),
        P("rep", "tp"),
        P("rep", "tp"),
        P("rep", "tp"),
        P("rep", "tp"),
        P("rep", "tp"),
    )
    return jax.shard_map(
        on_device,
        mesh=mesh,
        in_specs=placed,
        out_specs=(P("rep", "tp"), P("rep", "tp"), P("rep", "tp"), P("rep", "tp")),
        check_vma=False,
    )
```

```python
import functools
import math

import jax
import jax.numpy as jnp
from jax import lax
from jax.experimental import pallas as pl
from jax.experimental.pallas import tpu as pltpu
from jax.sharding import PartitionSpec as P

beta_one = 0.9
beta_two = 0.95
bias_one = 1.0 - 0.9**10
bias_two = 1.0 - 0.95**10
learn_rate = 0.05
weight_decay = 0.1
epsilon = 1e-08

D, TOK, WIDE, UNIT, NARROW = 4096, 384, 896, 128, 1024
REP, TP = 8, 16
OWN, SHARE = 96, 256
ROWS = D // REP
STRIP = ROWS // TP
SEVEN = WIDE // UNIT
PART = TOK // (TP // 2)
KINDS = REP // 2
SCALING = 1.0 / math.sqrt(D)
MESH = pl.DeviceIdType.MESH
F32, BF16 = jnp.float32, jnp.bfloat16


class Place:
    def __init__(self):
        r, t = lax.axis_index("rep"), lax.axis_index("tp")
        self.r, self.t = r, t
        x, zl = r % 4, r // 4
        y, zh, c = t // 4, (t // 2) % 2, t % 2
        self.core = c
        self.chip = t // 2
        self.sibling = (r, t + 1 - 2 * c)

        def rep_id(step, flip):
            return (x + step) % 4 + 4 * ((zl + flip) % 2)

        def tp_id(step, flip):
            return ((y + step) % 4) * 4 + ((zh + flip) % 2) * 2 + c

        self.rep_ids = [[rep_id(s, f) for s in (0, 1, 3, 2)] for f in (0, 1)]
        self.tp_ids = [[tp_id(s, f) for s in (0, 1, 3, 2)] for f in (0, 1)]

    def rep_dev(self, other):
        return (other, self.t)

    def tp_dev(self, other):
        return (self.r, other)


def greet(place):
    barrier = pltpu.get_barrier_semaphore()

    def rep_mate(k, carry):
        pl.semaphore_signal(barrier, inc=1, device_id=((place.r + k) % REP, place.t), device_id_type=MESH)
        return carry

    def tp_mate(k, carry):
        pl.semaphore_signal(barrier, inc=1, device_id=(place.r, (place.t + k) % TP), device_id_type=MESH)
        return carry

    lax.fori_loop(1, REP, rep_mate, 0)
    lax.fori_loop(1, TP, tp_mate, 0)
    pl.semaphore_wait(barrier, REP + TP - 2)


class Tree:
    def __init__(self, view, ids, dev, ssem, rsem, extent, first):
        (me, nx, pv, op), (me_p, nx_p, pv_p, op_p) = ids
        to_nx, to_pv, to_pair = dev(nx), dev(pv), dev(me_p)
        half, a_half, rest = extent // 2, first // 2, extent - first
        self.rest, self.names = rest, dict(me=me, nx=nx, pv=pv, op=op, me_p=me_p, nx_p=nx_p, pv_p=pv_p, op_p=op_p)
        sent = {
            1: (me, 0, extent, to_nx), 2: (me, 0, extent, to_pv), 3: (me, 0, first, to_pair), 4: (me, first, rest, to_pair),
            5: (me_p, 0, first, to_nx), 6: (me_p, 0, first, to_pv), 7: (pv, 0, half, to_nx), 8: (nx, half, half, to_pv),
            9: (pv_p, 0, a_half, to_nx), 10: (nx_p, a_half, a_half, to_pv),
            11: (pv, first, rest, to_pair), 12: (nx, first, rest, to_pair), 13: (op, first, rest, to_pair),
        }
        got = {1: pv, 2: nx, 3: me_p, 4: me_p, 5: pv_p, 6: nx_p, 7: op, 8: op, 9: op_p, 10: op_p, 11: pv_p, 12: nx_p, 13: op_p}
        skipped = () if rest else (4, 11, 12, 13)
        self.out, self.into = {}, {}
        for i, (chunk, low, count, to) in sent.items():
            if i not in skipped:
                for book, which in ((self.out, chunk), (self.into, got[i])):
                    ref = view(which, low, count)
                    book[i] = pltpu.make_async_remote_copy(
                        src_ref=ref, dst_ref=ref, send_sem=ssem.at[i - 1], recv_sem=rsem.at[i - 1],
                        device_id=to, device_id_type=MESH,
                    )

    def start(self, *which):
        for i in which:
            if i in self.out:
                self.out[i].start()

    def wait(self, *which):
        for i in which:
            if i in self.into:
                self.into[i].wait_recv()

    def steps(self, done):
        def pair():
            self.wait(3)
            self.start(5, 6)
            if not self.rest:
                done("me_p")

        def previous():
            self.wait(1)
            self.start(7, 11)
            done("pv")

        def following():
            self.wait(2)
            self.start(8, 12)
            done("nx")

        def pair_previous():
            self.wait(5)
            self.start(9)
            if not self.rest:
                done("pv_p")

        def pair_following():
            self.wait(6)
            self.start(10)
            if not self.rest:
                done("nx_p")

        def opposite():
            self.wait(7, 8)
            self.start(13)
            done("op")

        def rests():
            if self.rest:
                self.wait(4)
                done("me_p")
                self.wait(11)
                done("pv_p")
                self.wait(12)
                done("nx_p")

        def last():
            self.wait(9, 10, 13)
            done("op_p")

        return [pair, previous, following, pair_previous, pair_following, opposite, rests, last]

    def begin(self):
        self.start(3, 1, 2, 4)

    def drain(self):
        for copy in self.out.values():
            copy.wait_send()


ORDER = ("me", "pv", "nx", "me_p", "op", "pv_p", "nx_p", "op_p")


class Siblings:
    def __init__(self, tree, view, extent, place, ssem, rsem):
        self.out, self.into = {}, {}
        for n, name in enumerate(ORDER):
            mine = tree.names[name]
            for book, which in ((self.out, mine), (self.into, mine + 1 - 2 * place.core)):
                ref = view(which, 0, extent)
                book[name] = pltpu.make_async_remote_copy(
                    src_ref=ref, dst_ref=ref, send_sem=ssem.at[n], recv_sem=rsem.at[n],
                    device_id=place.sibling, device_id_type=MESH,
                )

    def start(self, name):
        self.out[name].start()

    def wait(self, name):
        self.into[name].wait_recv()

    def drain(self):
        for copy in self.out.values():
            copy.wait_send()


def step_kernel(
    rows_ref, slots_ref, holders_ref, map_ref, copies_ref, upstream_ref, act_ref, master_ref, one_ref, two_ref,
    master_out, one_out, two_out, full_out, adopted_out, maps_out,
    own_rows, spread, inputs, weight, gates, upstream, act, grad, pieces,
    parts, grads, total, fresh, strips, strewn, picked, routed, outgoing, adopted, master, one, two, maps,
    map_s, map_r, row_s, row_r, tree_s, tree_r, sib_s, sib_r, tree2_s, tree2_r, sib2_s, sib2_r,
    swap_s, swap_r, part_s, part_r, sib3_s, sib3_r, grad_s, grad_r, fresh_s, fresh_r,
    p1_s, p1_r, p2_s, p2_r, p3_s, p3_r, local, outs,
):
    place = Place()
    r, t = place.r, place.t

    def loading(n, source, target):
        copy = pltpu.make_async_copy(source, target, local.at[n])
        copy.start()
        return copy

    load_rows = loading(0, rows_ref, own_rows)
    load_weight = loading(1, copies_ref, weight)
    load_factors = [loading(2, upstream_ref, upstream), loading(3, act_ref, act)]
    load_state = [loading(4, master_ref, master), loading(5, one_ref, one), loading(6, two_ref, two)]
    own_map = loading(7, map_ref, maps_out.at[r])
    greet(place)
    load_rows.wait()

    def each(count, act_on):
        lax.fori_loop(1, count, lambda k, c: (act_on(k), c)[1], 0)

    def remote(source, target, s, r_, k, to):
        return pltpu.make_async_remote_copy(
            src_ref=source, dst_ref=target, send_sem=s.at[k], recv_sem=r_.at[k], device_id=to, device_id_type=MESH
        )

    def share_to(k):
        to = (t + k) % TP
        return remote(
            own_rows.at[:, pl.ds(pl.multiple_of(to * SHARE, SHARE), SHARE)],
            spread.at[pl.ds(pl.multiple_of(t * OWN, OWN), OWN), :], row_s, row_r, k, (r, to),
        )

    def share_from(k):
        source = (t + TP - k) % TP
        ref = spread.at[pl.ds(pl.multiple_of(source * OWN, OWN), OWN), :]
        return remote(ref, ref, row_s, row_r, k, (r, source))

    each(TP, lambda k: share_to(k).start())
    own_share = loading(
        8, own_rows.at[:, pl.ds(pl.multiple_of(t * SHARE, SHARE), SHARE)],
        spread.at[pl.ds(pl.multiple_of(t * OWN, OWN), OWN), :],
    )

    def map_to(k):
        return remote(map_ref, maps_out.at[r], map_s, map_r, k, ((r + k) % REP, t))

    def map_from(k):
        source = (r + REP - k) % REP
        return remote(map_ref, maps_out.at[source], map_s, map_r, k, (source, t))

    each(REP, lambda k: map_to(k).start())
    own_share.wait()
    each(TP, lambda k: share_from(k).wait_recv())

    slots = slots_ref[...]
    found = jnp.zeros((TOK, SHARE), F32)
    block = 512
    for b in range(TP * OWN // block):
        places = lax.broadcasted_iota(jnp.int32, (TOK, block), 1) + b * block
        one_hot = jnp.where(slots == places, 1.0, 0.0).astype(BF16)
        found += jnp.dot(one_hot, spread[b * block : (b + 1) * block, :], preferred_element_type=F32)
    inputs[t] = found.astype(BF16)

    def input_view(chunk, low, count):
        return inputs.at[chunk, pl.ds(low, count), :]

    tree = Tree(input_view, place.tp_ids, place.tp_dev, tree_s, tree_r, TOK, 224)
    sibs = Siblings(tree, input_view, TOK, place, sib_s, sib_r)
    tree.begin()
    sibs.start("me")
    load_weight.wait()

    def multiplied(chunk, first=False):
        depth = pl.ds(pl.multiple_of(chunk * SHARE, SHARE), SHARE)
        for n in range(4):
            cols = slice(n * 256, (n + 1) * 256)
            part = jnp.dot(inputs[chunk], weight[depth, cols], preferred_element_type=F32)
            gates[:, cols] = part if first else gates[:, cols] + part

    def other_multiplied(name):
        sibs.wait(name)
        multiplied(tree.names[name] + 1 - 2 * place.core)

    multiplied(t, True)
    waiting = ["me"]

    def whole(name):
        sibs.start(name)
        multiplied(tree.names[name])
        waiting.append(name)
        if len(waiting) > 2:
            other_multiplied(waiting.pop(0))

    for step in tree.steps(whole):
        step()
    for name in waiting:
        other_multiplied(name)

    mine_rows = pl.ds(pl.multiple_of(place.chip * PART, PART), PART)
    mine_cols = pl.ds(pl.multiple_of(place.core * SHARE, SHARE), SHARE)

    def swap_to(k):
        to = (r + k) % REP
        return remote(
            inputs.at[2 * to + place.core, mine_rows, :], parts.at[r, mine_rows, mine_cols], swap_s, swap_r, k, (to, t)
        )

    def swap_from(k):
        source = (r + REP - k) % REP
        ref = parts.at[source, mine_rows, mine_cols]
        return remote(ref, ref, swap_s, swap_r, k, (source, t))

    each(REP, lambda k: swap_to(k).start())
    own_swap = loading(9, inputs.at[2 * r + place.core, mine_rows, :], parts.at[r, mine_rows, mine_cols])

    for load in load_factors:
        load.wait()

    def gate_rows(n, carry):
        at = pl.ds(pl.multiple_of(n * 16, 16), 16)
        gate = gates[at, :] * SCALING
        logistic = 1.0 / (1.0 + jnp.exp(-gate))
        grad[at, :] = (
            upstream[at, :].astype(F32) * act[at, :].astype(F32) * logistic * (1.0 + gate * (1.0 - logistic))
        ).astype(BF16)
        return carry

    lax.fori_loop(0, TOK // 16, gate_rows, 0)
    pieces[t] = grad[:, WIDE:]

    def piece_view(chunk, low, count):
        return pieces.at[chunk, pl.ds(low, count), :]

    tree2 = Tree(piece_view, place.tp_ids, place.tp_dev, tree2_s, tree2_r, TOK, TOK)
    sibs2 = Siblings(tree2, piece_view, TOK, place, sib2_s, sib2_r)
    tree2.begin()
    sibs2.start("me")
    for step in tree2.steps(sibs2.start):
        step()
    own_swap.wait()
    each(REP, lambda k: swap_from(k).wait_recv())
    for name in ORDER:
        sibs2.wait(name)

    own_entry = holders_ref[0, t]
    for s in range(SEVEN):
        wanted = t * SEVEN + s
        owner = jnp.int32(0)
        for other in range(TP):
            owner = jnp.where(holders_ref[0, other] == wanted, other, owner)
        cols = slice(s * UNIT, (s + 1) * UNIT)
        grads[r, :, cols] = jnp.where(own_entry == -2, pieces[owner], grad[:, cols])

    def grad_view(chunk, low, count):
        return grads.at[chunk, pl.ds(low, count), :]

    gtree = Tree(grad_view, place.rep_ids, place.rep_dev, grad_s, grad_r, TOK, 224)
    gtree.begin()

    def part_view(chunk, low, count):
        at, side = chunk // 2, chunk % 2
        return parts.at[
            pl.ds(low, count),
            pl.ds(pl.multiple_of(at * PART, PART), PART),
            pl.ds(pl.multiple_of(side * SHARE, SHARE), SHARE),
        ]

    ptree = Tree(part_view, place.tp_ids, place.tp_dev, part_s, part_r, REP, REP)
    sibs3 = Siblings(ptree, part_view, REP, place, sib3_s, sib3_r)
    ptree.begin()
    sibs3.start("me")

    def gathered(chunk, first=False):
        part = lax.dot_general(
            parts[chunk], grads[chunk], (((0,), (0,)), ((), ())), preferred_element_type=F32
        )
        total[...] = part if first else total[...] + part

    own_map.wait()
    each(REP, lambda k: map_from(k).wait_recv())
    load_maps = loading(10, maps_out, maps)
    gsteps = gtree.steps(lambda name: gathered(gtree.names[name]))
    psteps = ptree.steps(sibs3.start)
    for step in psteps[:5]:
        step()
    gsteps[0]()
    for step in psteps[5:]:
        step()
    for name in ORDER:
        sibs3.wait(name)
    gathered(r, True)
    for step in gsteps[1:]:
        step()

    for load in load_state:
        load.wait()

    def adam_rows(n, carry):
        at = pl.ds(pl.multiple_of(n * 16, 16), 16)
        gradient = total[at, :] * SCALING
        first_new = beta_one * one[at, :].astype(F32) + (1.0 - beta_one) * gradient
        second_new = beta_two * two[at, :].astype(F32) + (1.0 - beta_two) * gradient * gradient
        step_size = first_new / bias_one / (jnp.sqrt(second_new / bias_two) + epsilon)
        old = master[at, :]
        new = old - learn_rate * (step_size + weight_decay * old)
        master[at, :] = new
        one[at, :] = first_new.astype(BF16)
        two[at, :] = second_new.astype(BF16)
        low = new.astype(BF16)
        fresh[r, at, :] = low
        for s in range(SEVEN):
            strips[s, at, :] = low[:, s * UNIT : (s + 1) * UNIT]
        return carry

    lax.fori_loop(0, ROWS // 16, adam_rows, 0)

    def fresh_view(chunk, low, count):
        return fresh.at[chunk, pl.ds(low, count), :]

    ftree = Tree(fresh_view, place.rep_ids, place.rep_dev, fresh_s, fresh_r, ROWS, 384)

    def strip_of(device):
        return pl.ds(pl.multiple_of(device * STRIP, STRIP), STRIP)

    def one_to(k):
        to = (t + k) % TP
        return remote(strips.at[:, strip_of(to), :], strewn.at[pl.ds(t * SEVEN, SEVEN)], p1_s, p1_r, k, (r, to))

    def one_from(k):
        source = (t + TP - k) % TP
        ref = strewn.at[pl.ds(source * SEVEN, SEVEN)]
        return remote(ref, ref, p1_s, p1_r, k, (r, source))

    each(TP, lambda k: one_to(k).start())
    ftree.begin()
    strewn[pl.ds(t * SEVEN, SEVEN)] = strips[:, strip_of(t), :]
    stores = []

    def storing(source, target):
        copy = pltpu.make_async_copy(source, target, outs.at[len(stores)])
        copy.start()
        stores.append(copy)

    storing(master, master_out)
    storing(one, one_out)
    storing(two, two_out)
    storing(fresh.at[r], full_out.at[r])

    load_maps.wait()
    narrow, rank, count = [], [], jnp.int32(0)
    for q in range(REP):
        narrow.append(maps[q, 0, 0] != -1)
        rank.append(jnp.minimum(count, KINDS - 1))
        count = count + jnp.where(narrow[q], 1, 0)
    which = []
    for k in range(KINDS):
        chosen = jnp.int32(0)
        for q in range(REP):
            chosen = jnp.where(narrow[q] & (rank[q] == k), q, chosen)
        which.append(chosen)

    each(TP, lambda k: one_from(k).wait_recv())
    for k in range(KINDS):

        def pick(to, carry, k=k):
            piece = maps[which[k], 0, to]
            value = strewn[jnp.maximum(piece, 0)]
            picked[to, k] = jnp.where(piece >= 0, value, jnp.zeros_like(value))
            return carry

        lax.fori_loop(0, TP, pick, 0)

    def two_to(k):
        to = (t + k) % TP
        return remote(picked.at[to], routed.at[:, strip_of(t), :], p2_s, p2_r, k, (r, to))

    def two_from(k):
        source = (t + TP - k) % TP
        ref = routed.at[:, strip_of(source), :]
        return remote(ref, ref, p2_s, p2_r, k, (r, source))

    each(TP, lambda k: two_to(k).start())
    routed[:, strip_of(t), :] = picked[t]

    def stored(name):
        chunk = ftree.names[name]
        storing(fresh.at[chunk], full_out.at[chunk])

    fsteps = ftree.steps(stored)
    for step in fsteps[:1]:
        step()
    each(TP, lambda k: two_from(k).wait_recv())
    for q in range(REP):
        value = routed[rank[q]]
        outgoing[q] = jnp.where(narrow[q], value, jnp.zeros_like(value))

    def three_to(k):
        to = (r + k) % REP
        return remote(outgoing.at[to], adopted.at[r], p3_s, p3_r, k, (to, t))

    def three_from(k):
        source = (r + REP - k) % REP
        return remote(adopted.at[source], adopted.at[source], p3_s, p3_r, k, (source, t))

    each(REP, lambda k: three_to(k).start())
    adopted[r] = outgoing[r]
    for step in fsteps[1:]:
        step()
    each(REP, lambda k: three_from(k).wait_recv())
    storing(adopted, adopted_out)

    for book in (tree, sibs, tree2, sibs2, ptree, sibs3, gtree, ftree):
        book.drain()
    each(REP, lambda k: map_to(k).wait_send())
    each(TP, lambda k: share_to(k).wait_send())
    each(REP, lambda k: swap_to(k).wait_send())
    each(TP, lambda k: one_to(k).wait_send())
    each(TP, lambda k: two_to(k).wait_send())
    each(REP, lambda k: three_to(k).wait_send())
    for store in stores:
        store.wait()


ANY = pl.BlockSpec(memory_space=pl.ANY)
VM = pl.BlockSpec(memory_space=pltpu.VMEM)
SM = pl.BlockSpec(memory_space=pltpu.SMEM)


def sems(*counts):
    return [pltpu.SemaphoreType.DMA((n,)) for n in counts for _ in (0, 1)]


def on_device(
    batch_rows, token_slots, holder_map, copies, upstream, up_act, master, moment1, moment2
):
    own_entry = jnp.sum(jnp.where(jnp.arange(TP) == lax.axis_index("tp"), holder_map[0], 0))
    master_next, one_next, two_next, full, adopted, _ = pl.pallas_call(
        step_kernel,
        out_shape=(
            jax.ShapeDtypeStruct((ROWS, WIDE), F32),
            jax.ShapeDtypeStruct((ROWS, WIDE), BF16),
            jax.ShapeDtypeStruct((ROWS, WIDE), BF16),
            jax.ShapeDtypeStruct((REP, ROWS, WIDE), BF16),
            jax.ShapeDtypeStruct((REP, ROWS, UNIT), BF16),
            jax.ShapeDtypeStruct((REP, 1, TP), jnp.int32),
        ),
        in_specs=[ANY, VM, SM, ANY, ANY, ANY, ANY, ANY, ANY, ANY],
        out_specs=(ANY,) * 6,
        scratch_shapes=[
            pltpu.VMEM((OWN, D), BF16),
            pltpu.VMEM((TP * OWN, SHARE), BF16),
            pltpu.VMEM((TP, TOK, SHARE), BF16),
            pltpu.VMEM((D, NARROW), BF16),
            pltpu.VMEM((TOK, NARROW), F32),
            pltpu.VMEM((TOK, NARROW), BF16),
            pltpu.VMEM((TOK, NARROW), BF16),
            pltpu.VMEM((TOK, NARROW), BF16),
            pltpu.VMEM((TP, TOK, UNIT), BF16),
            pltpu.VMEM((REP, TOK, ROWS), BF16),
            pltpu.VMEM((REP, TOK, WIDE), BF16),
            pltpu.VMEM((ROWS, WIDE), F32),
            pltpu.VMEM((REP, ROWS, WIDE), BF16),
            pltpu.VMEM((SEVEN, ROWS, UNIT), BF16),
            pltpu.VMEM((TP * SEVEN, STRIP, UNIT), BF16),
            pltpu.VMEM((TP, KINDS, STRIP, UNIT), BF16),
            pltpu.VMEM((KINDS, ROWS, UNIT), BF16),
            pltpu.VMEM((REP, ROWS, UNIT), BF16),
            pltpu.VMEM((REP, ROWS, UNIT), BF16),
            pltpu.VMEM((ROWS, WIDE), F32),
            pltpu.VMEM((ROWS, WIDE), BF16),
            pltpu.VMEM((ROWS, WIDE), BF16),
            pltpu.SMEM((REP, 1, TP), jnp.int32),
            *sems(REP, TP, 13, 8, 13, 8),
            *sems(REP, 13, 8, 13, 13, TP, TP, REP),
            pltpu.SemaphoreType.DMA((11,)),
            pltpu.SemaphoreType.DMA((12,)),
        ],
        compiler_params=pltpu.CompilerParams(
            collective_id=0, has_side_effects=True, vmem_limit_bytes=60 << 20
        ),
        name="step",
    )(
        batch_rows, token_slots.reshape(TOK, 1), holder_map, holder_map, copies, upstream, up_act,
        master, moment1, moment2,
    )
    copy_next = jnp.concatenate([full.reshape(D, WIDE), adopted.reshape(D, UNIT)], axis=1)
    copy_next = jnp.where(own_entry == -2, jnp.zeros_like(copy_next), copy_next)
    return master_next, one_next, two_next, copy_next


def solution(mesh):
    placed = (
        P(("rep", "tp"), None),
        P("rep", None),
        P("rep", None),
        P("rep", "tp"),
        P("rep", "tp"),
        P("rep", "tp"),
        P("rep", "tp"),
        P("rep", "tp"),
        P("rep", "tp"),
    )
    return jax.shard_map(
        on_device,
        mesh=mesh,
        in_specs=placed,
        out_specs=(P("rep", "tp"), P("rep", "tp"), P("rep", "tp"), P("rep", "tp")),
        check_vma=False,
    )
```

```python
import functools
import math

import jax
import jax.numpy as jnp
from jax import lax
from jax.experimental import pallas as pl
from jax.experimental.pallas import tpu as pltpu
from jax.sharding import PartitionSpec as P

beta_one = 0.9
beta_two = 0.95
bias_one = 1.0 - 0.9**10
bias_two = 1.0 - 0.95**10
learn_rate = 0.05
weight_decay = 0.1
epsilon = 1e-08

D, TOK, WIDE, UNIT, NARROW = 4096, 384, 896, 128, 1024
REP, TP = 8, 16
OWN, SHARE = 96, 256
ROWS = D // REP
STRIP = ROWS // TP
SEVEN = WIDE // UNIT
PART = TOK // (TP // 2)
KINDS = REP // 2
SCALING = 1.0 / math.sqrt(D)
MESH = pl.DeviceIdType.MESH
F32, BF16 = jnp.float32, jnp.bfloat16


class Place:
    def __init__(self):
        r, t = lax.axis_index("rep"), lax.axis_index("tp")
        self.r, self.t = r, t
        x, zl = r % 4, r // 4
        y, zh, c = t // 4, (t // 2) % 2, t % 2
        self.core = c
        self.chip = t // 2
        self.sibling = (r, t + 1 - 2 * c)

        def rep_id(step, flip):
            return (x + step) % 4 + 4 * ((zl + flip) % 2)

        def tp_id(step, flip):
            return ((y + step) % 4) * 4 + ((zh + flip) % 2) * 2 + c

        self.rep_ids = [[rep_id(s, f) for s in (0, 1, 3, 2)] for f in (0, 1)]
        self.tp_ids = [[tp_id(s, f) for s in (0, 1, 3, 2)] for f in (0, 1)]

    def rep_dev(self, other):
        return (other, self.t)

    def tp_dev(self, other):
        return (self.r, other)


def greet(place):
    barrier = pltpu.get_barrier_semaphore()

    def rep_mate(k, carry):
        pl.semaphore_signal(barrier, inc=1, device_id=((place.r + k) % REP, place.t), device_id_type=MESH)
        return carry

    def tp_mate(k, carry):
        pl.semaphore_signal(barrier, inc=1, device_id=(place.r, (place.t + k) % TP), device_id_type=MESH)
        return carry

    lax.fori_loop(1, REP, rep_mate, 0)
    lax.fori_loop(1, TP, tp_mate, 0)
    pl.semaphore_wait(barrier, REP + TP - 2)


class Tree:
    def __init__(self, view, ids, dev, ssem, rsem, extent, first):
        (me, nx, pv, op), (me_p, nx_p, pv_p, op_p) = ids
        to_nx, to_pv, to_pair = dev(nx), dev(pv), dev(me_p)
        half, a_half, rest = extent // 2, first // 2, extent - first
        self.rest, self.names = rest, dict(me=me, nx=nx, pv=pv, op=op, me_p=me_p, nx_p=nx_p, pv_p=pv_p, op_p=op_p)
        sent = {
            1: (me, 0, extent, to_nx), 2: (me, 0, extent, to_pv), 3: (me, 0, first, to_pair), 4: (me, first, rest, to_pair),
            5: (me_p, 0, first, to_nx), 6: (me_p, 0, first, to_pv), 7: (pv, 0, half, to_nx), 8: (nx, half, half, to_pv),
            9: (pv_p, 0, a_half, to_nx), 10: (nx_p, a_half, a_half, to_pv),
            11: (pv, first, rest, to_pair), 12: (nx, first, rest, to_pair), 13: (op, first, rest, to_pair),
        }
        got = {1: pv, 2: nx, 3: me_p, 4: me_p, 5: pv_p, 6: nx_p, 7: op, 8: op, 9: op_p, 10: op_p, 11: pv_p, 12: nx_p, 13: op_p}
        skipped = () if rest else (4, 11, 12, 13)
        self.out, self.into = {}, {}
        for i, (chunk, low, count, to) in sent.items():
            if i not in skipped:
                for book, which in ((self.out, chunk), (self.into, got[i])):
                    ref = view(which, low, count)
                    book[i] = pltpu.make_async_remote_copy(
                        src_ref=ref, dst_ref=ref, send_sem=ssem.at[i - 1], recv_sem=rsem.at[i - 1],
                        device_id=to, device_id_type=MESH,
                    )

    def start(self, *which):
        for i in which:
            if i in self.out:
                self.out[i].start()

    def wait(self, *which):
        for i in which:
            if i in self.into:
                self.into[i].wait_recv()

    def steps(self, done):
        def pair():
            self.wait(3)
            self.start(5, 6)
            if not self.rest:
                done("me_p")

        def previous():
            self.wait(1)
            self.start(7, 11)
            done("pv")

        def following():
            self.wait(2)
            self.start(8, 12)
            done("nx")

        def pair_previous():
            self.wait(5)
            self.start(9)
            if not self.rest:
                done("pv_p")

        def pair_following():
            self.wait(6)
            self.start(10)
            if not self.rest:
                done("nx_p")

        def opposite():
            self.wait(7, 8)
            self.start(13)
            done("op")

        def rests():
            if self.rest:
                self.wait(4)
                done("me_p")
                self.wait(11)
                done("pv_p")
                self.wait(12)
                done("nx_p")

        def last():
            self.wait(9, 10, 13)
            done("op_p")

        return [pair, previous, following, pair_previous, pair_following, opposite, rests, last]

    def begin(self):
        self.start(3, 1, 2, 4)

    def drain(self):
        for copy in self.out.values():
            copy.wait_send()


ORDER = ("me", "pv", "nx", "me_p", "op", "pv_p", "nx_p", "op_p")


class Siblings:
    def __init__(self, tree, view, extent, place, ssem, rsem):
        self.out, self.into = {}, {}
        for n, name in enumerate(ORDER):
            mine = tree.names[name]
            for book, which in ((self.out, mine), (self.into, mine + 1 - 2 * place.core)):
                ref = view(which, 0, extent)
                book[name] = pltpu.make_async_remote_copy(
                    src_ref=ref, dst_ref=ref, send_sem=ssem.at[n], recv_sem=rsem.at[n],
                    device_id=place.sibling, device_id_type=MESH,
                )

    def start(self, name):
        self.out[name].start()

    def wait(self, name):
        self.into[name].wait_recv()

    def drain(self):
        for copy in self.out.values():
            copy.wait_send()


def step_kernel(
    rows_ref, slots_ref, holders_ref, map_ref, copies_ref, upstream_ref, act_ref, master_ref, one_ref, two_ref,
    master_out, one_out, two_out, full_out, adopted_out, maps_out,
    own_rows, spread, inputs, choice, weight, gates, upstream, act, grad, pieces,
    parts, grads, total, fresh, strips, strewn, picked, routed, outgoing, adopted, master, one, two, maps,
    map_s, map_r, row_s, row_r, tree_s, tree_r, sib_s, sib_r, tree2_s, tree2_r, sib2_s, sib2_r,
    swap_s, swap_r, part_s, part_r, sib3_s, sib3_r, grad_s, grad_r, fresh_s, fresh_r,
    p1_s, p1_r, p2_s, p2_r, p3_s, p3_r, local, outs,
):
    place = Place()
    r, t = place.r, place.t

    def loading(n, source, target):
        copy = pltpu.make_async_copy(source, target, local.at[n])
        copy.start()
        return copy

    load_rows = loading(0, rows_ref, own_rows)
    load_weight = loading(1, copies_ref, weight)
    load_factors = [loading(2, upstream_ref, upstream), loading(3, act_ref, act)]
    load_state = [loading(4, master_ref, master), loading(5, one_ref, one), loading(6, two_ref, two)]
    own_map = loading(7, map_ref, maps_out.at[r])
    greet(place)
    load_rows.wait()

    def each(count, act_on):
        lax.fori_loop(1, count, lambda k, c: (act_on(k), c)[1], 0)

    def remote(source, target, s, r_, k, to):
        return pltpu.make_async_remote_copy(
            src_ref=source, dst_ref=target, send_sem=s.at[k], recv_sem=r_.at[k], device_id=to, device_id_type=MESH
        )

    def columns_of(device):
        return pl.ds(pl.multiple_of(device * SHARE, SHARE), SHARE)

    def share_to(k):
        to = (t + k) % TP
        return remote(
            own_rows.at[:, pl.ds(pl.multiple_of(to * SHARE, SHARE), SHARE)],
            spread.at[pl.ds(pl.multiple_of(t * OWN, OWN), OWN), :], row_s, row_r, k, (r, to),
        )

    def share_from(k):
        source = (t + TP - k) % TP
        ref = spread.at[pl.ds(pl.multiple_of(source * OWN, OWN), OWN), :]
        return remote(ref, ref, row_s, row_r, k, (r, source))

    each(TP, lambda k: share_to(k).start())
    own_share = loading(
        8, own_rows.at[:, pl.ds(pl.multiple_of(t * SHARE, SHARE), SHARE)],
        spread.at[pl.ds(pl.multiple_of(t * OWN, OWN), OWN), :],
    )

    def map_to(k):
        return remote(map_ref, maps_out.at[r], map_s, map_r, k, ((r + k) % REP, t))

    def map_from(k):
        source = (r + REP - k) % REP
        return remote(map_ref, maps_out.at[source], map_s, map_r, k, (source, t))

    each(REP, lambda k: map_to(k).start())
    def choose(n, carry):
        at = pl.ds(pl.multiple_of(n * 16, 16), 16)
        places = lax.broadcasted_iota(jnp.int32, (16, TP * OWN), 1)
        choice[at, :] = jnp.where(slots_ref[at, :] == places, 1.0, 0.0).astype(BF16)
        return carry

    lax.fori_loop(0, TOK // 16, choose, 0)
    own_share.wait()
    each(TP, lambda k: share_from(k).wait_recv())

    inputs[:, columns_of(t)] = jnp.dot(choice[...], spread[...], preferred_element_type=F32).astype(BF16)

    def input_view(chunk, low, count):
        return inputs.at[pl.ds(low, count), columns_of(chunk)]

    tree = Tree(input_view, place.tp_ids, place.tp_dev, tree_s, tree_r, TOK, 224)
    sibs = Siblings(tree, input_view, TOK, place, sib_s, sib_r)
    tree.begin()
    sibs.start("me")
    load_weight.wait()

    def multiplied(name, first=False):
        sibs.wait(name)
        depth = pl.ds(pl.multiple_of(tree.names[name] // 2 * (2 * SHARE), 2 * SHARE), 2 * SHARE)
        for n in range(2):
            cols = slice(n * 512, (n + 1) * 512)
            part = jnp.dot(inputs[:, depth], weight[depth, cols], preferred_element_type=F32)
            gates[:, cols] = part if first else gates[:, cols] + part

    waiting = ["me"]

    def whole(name):
        sibs.start(name)
        waiting.append(name)
        if len(waiting) > 2:
            before = waiting.pop(0)
            multiplied(before, before == "me")

    for step in tree.steps(whole):
        step()
    for name in waiting:
        multiplied(name)

    mine_rows = pl.ds(pl.multiple_of(place.chip * PART, PART), PART)
    mine_cols = pl.ds(pl.multiple_of(place.core * SHARE, SHARE), SHARE)

    def swap_to(k):
        to = (r + k) % REP
        return remote(
            inputs.at[mine_rows, columns_of(2 * to + place.core)], parts.at[r, mine_rows, mine_cols], swap_s, swap_r, k, (to, t)
        )

    def swap_from(k):
        source = (r + REP - k) % REP
        ref = parts.at[source, mine_rows, mine_cols]
        return remote(ref, ref, swap_s, swap_r, k, (source, t))

    each(REP, lambda k: swap_to(k).start())
    own_swap = loading(9, inputs.at[mine_rows, columns_of(2 * r + place.core)], parts.at[r, mine_rows, mine_cols])

    for load in load_factors:
        load.wait()

    def gate_rows(tall, cols, keep):
        def rows(n, carry):
            at = pl.ds(pl.multiple_of(n * tall, tall), tall)
            gate = gates[at, cols] * SCALING
            logistic = 1.0 / (1.0 + jnp.exp(-gate))
            factors = upstream[at, cols].astype(F32) * act[at, cols].astype(F32)
            keep(at, (factors * logistic * (1.0 + gate * (1.0 - logistic))).astype(BF16))
            return carry

        lax.fori_loop(0, TOK // tall, rows, 0)

    def keep_piece(at, value):
        pieces[t, at, :] = value

    def keep_wide(at, value):
        grad[at, :] = value

    gate_rows(64, slice(WIDE, NARROW), keep_piece)

    def piece_view(chunk, low, count):
        return pieces.at[chunk, pl.ds(low, count), :]

    tree2 = Tree(piece_view, place.tp_ids, place.tp_dev, tree2_s, tree2_r, TOK, TOK)
    sibs2 = Siblings(tree2, piece_view, TOK, place, sib2_s, sib2_r)
    tree2.begin()
    sibs2.start("me")
    gate_rows(16, slice(0, WIDE), keep_wide)

    def part_view(chunk, low, count):
        at, side = chunk // 2, chunk % 2
        return parts.at[
            pl.ds(low, count),
            pl.ds(pl.multiple_of(at * PART, PART), PART),
            pl.ds(pl.multiple_of(side * SHARE, SHARE), SHARE),
        ]

    ptree = Tree(part_view, place.tp_ids, place.tp_dev, part_s, part_r, REP, REP)
    sibs3 = Siblings(ptree, part_view, REP, place, sib3_s, sib3_r)
    steps2 = tree2.steps(sibs2.start)
    for step in steps2[:5]:
        step()
    own_swap.wait()
    each(REP, lambda k: swap_from(k).wait_recv())
    ptree.begin()
    sibs3.start("me")
    for step in steps2[5:]:
        step()
    for name in ORDER:
        sibs2.wait(name)

    own_entry = holders_ref[0, t]
    for s in range(SEVEN):
        wanted = t * SEVEN + s
        owner = jnp.int32(0)
        for other in range(TP):
            owner = jnp.where(holders_ref[0, other] == wanted, other, owner)
        cols = slice(s * UNIT, (s + 1) * UNIT)
        grads[r, :, cols] = jnp.where(own_entry == -2, pieces[owner], grad[:, cols])

    def grad_view(chunk, low, count):
        return grads.at[chunk, pl.ds(low, count), :]

    gtree = Tree(grad_view, place.rep_ids, place.rep_dev, grad_s, grad_r, TOK, 256)
    gtree.begin()

    def gathered(chunk, first=False):
        part = lax.dot_general(
            parts[chunk], grads[chunk], (((0,), (0,)), ((), ())), preferred_element_type=F32
        )
        total[...] = part if first else total[...] + part

    own_map.wait()
    each(REP, lambda k: map_from(k).wait_recv())
    load_maps = loading(10, maps_out, maps)
    gsteps = gtree.steps(lambda name: gathered(gtree.names[name]))
    for step in ptree.steps(sibs3.start):
        step()
    gsteps[0]()
    for name in ORDER:
        sibs3.wait(name)
    gathered(r, True)
    for step in gsteps[1:]:
        step()

    for load in load_state:
        load.wait()

    def strip_of(device):
        return pl.ds(pl.multiple_of(device * STRIP, STRIP), STRIP)

    def one_to(k):
        to = (t + k) % TP
        return remote(strips.at[:, strip_of(to), :], strewn.at[pl.ds(t * SEVEN, SEVEN)], p1_s, p1_r, k, (r, to))

    def adam_rows(n, carry):
        at = pl.ds(pl.multiple_of(n * 16, 16), 16)
        gradient = total[at, :] * SCALING
        first_new = beta_one * one[at, :].astype(F32) + (1.0 - beta_one) * gradient
        second_new = beta_two * two[at, :].astype(F32) + (1.0 - beta_two) * gradient * gradient
        step_size = first_new / bias_one / (jnp.sqrt(second_new / bias_two) + epsilon)
        old = master[at, :]
        new = old - learn_rate * (step_size + weight_decay * old)
        master[at, :] = new
        one[at, :] = first_new.astype(BF16)
        two[at, :] = second_new.astype(BF16)
        low = new.astype(BF16)
        fresh[r, at, :] = low
        for s in range(SEVEN):
            strips[s, at, :] = low[:, s * UNIT : (s + 1) * UNIT]
        return carry

    def strip_done(k, carry):
        to = (t + 1 + k) % TP
        lax.fori_loop(2 * to, 2 * to + 2, adam_rows, 0)

        @pl.when(k < TP - 1)
        def _():
            one_to(k + 1).start()

        return carry

    lax.fori_loop(0, TP, strip_done, 0)

    def fresh_view(chunk, low, count):
        return fresh.at[chunk, pl.ds(low, count), :]

    ftree = Tree(fresh_view, place.rep_ids, place.rep_dev, fresh_s, fresh_r, ROWS, 320)

    def one_from(k):
        source = (t + TP - k) % TP
        ref = strewn.at[pl.ds(source * SEVEN, SEVEN)]
        return remote(ref, ref, p1_s, p1_r, k, (r, source))

    ftree.begin()
    strewn[pl.ds(t * SEVEN, SEVEN)] = strips[:, strip_of(t), :]
    stores = []

    def storing(source, target):
        copy = pltpu.make_async_copy(source, target, outs.at[len(stores)])
        copy.start()
        stores.append(copy)

    storing(master, master_out)
    storing(one, one_out)
    storing(two, two_out)
    storing(fresh.at[r], full_out.at[r])

    load_maps.wait()
    narrow, rank, count = [], [], jnp.int32(0)
    for q in range(REP):
        narrow.append(maps[q, 0, 0] != -1)
        rank.append(jnp.minimum(count, KINDS - 1))
        count = count + jnp.where(narrow[q], 1, 0)
    which = []
    for k in range(KINDS):
        chosen = jnp.int32(0)
        for q in range(REP):
            chosen = jnp.where(narrow[q] & (rank[q] == k), q, chosen)
        which.append(chosen)

    each(TP, lambda k: one_from(k).wait_recv())
    for k in range(KINDS):

        def pick(to, carry, k=k):
            piece = maps[which[k], 0, to]
            value = strewn[jnp.maximum(piece, 0)]
            picked[to, k] = jnp.where(piece >= 0, value, jnp.zeros_like(value))
            return carry

        lax.fori_loop(0, TP, pick, 0)

    def two_to(k):
        to = (t + k) % TP
        return remote(picked.at[to], routed.at[:, strip_of(t), :], p2_s, p2_r, k, (r, to))

    def two_from(k):
        source = (t + TP - k) % TP
        ref = routed.at[:, strip_of(source), :]
        return remote(ref, ref, p2_s, p2_r, k, (r, source))

    each(TP, lambda k: two_to(k).start())
    routed[:, strip_of(t), :] = picked[t]

    def stored(name):
        chunk = ftree.names[name]
        storing(fresh.at[chunk], full_out.at[chunk])

    fsteps = ftree.steps(stored)
    for step in fsteps[:3]:
        step()
    each(TP, lambda k: two_from(k).wait_recv())
    for q in range(REP):
        value = routed[rank[q]]
        outgoing[q] = jnp.where(narrow[q], value, jnp.zeros_like(value))

    def three_to(k):
        to = (r + k) % REP
        return remote(outgoing.at[to], adopted.at[r], p3_s, p3_r, k, (to, t))

    def three_from(k):
        source = (r + REP - k) % REP
        return remote(adopted.at[source], adopted.at[source], p3_s, p3_r, k, (source, t))

    each(REP, lambda k: three_to(k).start())
    adopted[r] = outgoing[r]
    for step in fsteps[3:]:
        step()
    each(REP, lambda k: three_from(k).wait_recv())
    storing(adopted, adopted_out)

    for book in (tree, sibs, tree2, sibs2, ptree, sibs3, gtree, ftree):
        book.drain()
    each(REP, lambda k: map_to(k).wait_send())
    each(TP, lambda k: share_to(k).wait_send())
    each(REP, lambda k: swap_to(k).wait_send())
    each(TP, lambda k: one_to(k).wait_send())
    each(TP, lambda k: two_to(k).wait_send())
    each(REP, lambda k: three_to(k).wait_send())
    for store in stores:
        store.wait()


ANY = pl.BlockSpec(memory_space=pl.ANY)
VM = pl.BlockSpec(memory_space=pltpu.VMEM)
SM = pl.BlockSpec(memory_space=pltpu.SMEM)


def sems(*counts):
    return [pltpu.SemaphoreType.DMA((n,)) for n in counts for _ in (0, 1)]


def on_device(
    batch_rows, token_slots, holder_map, copies, upstream, up_act, master, moment1, moment2
):
    own_entry = jnp.sum(jnp.where(jnp.arange(TP) == lax.axis_index("tp"), holder_map[0], 0))
    master_next, one_next, two_next, full, adopted, _ = pl.pallas_call(
        step_kernel,
        out_shape=(
            jax.ShapeDtypeStruct((ROWS, WIDE), F32),
            jax.ShapeDtypeStruct((ROWS, WIDE), BF16),
            jax.ShapeDtypeStruct((ROWS, WIDE), BF16),
            jax.ShapeDtypeStruct((REP, ROWS, WIDE), BF16),
            jax.ShapeDtypeStruct((REP, ROWS, UNIT), BF16),
            jax.ShapeDtypeStruct((REP, 1, TP), jnp.int32),
        ),
        in_specs=[ANY, VM, SM, ANY, ANY, ANY, ANY, ANY, ANY, ANY],
        out_specs=(ANY,) * 6,
        scratch_shapes=[
            pltpu.VMEM((OWN, D), BF16),
            pltpu.VMEM((TP * OWN, SHARE), BF16),
            pltpu.VMEM((TOK, D), BF16),
            pltpu.VMEM((TOK, TP * OWN), BF16),
            pltpu.VMEM((D, NARROW), BF16),
            pltpu.VMEM((TOK, NARROW), F32),
            pltpu.VMEM((TOK, NARROW), BF16),
            pltpu.VMEM((TOK, NARROW), BF16),
            pltpu.VMEM((TOK, WIDE), BF16),
            pltpu.VMEM((TP, TOK, UNIT), BF16),
            pltpu.VMEM((REP, TOK, ROWS), BF16),
            pltpu.VMEM((REP, TOK, WIDE), BF16),
            pltpu.VMEM((ROWS, WIDE), F32),
            pltpu.VMEM((REP, ROWS, WIDE), BF16),
            pltpu.VMEM((SEVEN, ROWS, UNIT), BF16),
            pltpu.VMEM((TP * SEVEN, STRIP, UNIT), BF16),
            pltpu.VMEM((TP, KINDS, STRIP, UNIT), BF16),
            pltpu.VMEM((KINDS, ROWS, UNIT), BF16),
            pltpu.VMEM((REP, ROWS, UNIT), BF16),
            pltpu.VMEM((REP, ROWS, UNIT), BF16),
            pltpu.VMEM((ROWS, WIDE), F32),
            pltpu.VMEM((ROWS, WIDE), BF16),
            pltpu.VMEM((ROWS, WIDE), BF16),
            pltpu.SMEM((REP, 1, TP), jnp.int32),
            *sems(REP, TP, 13, 8, 13, 8),
            *sems(REP, 13, 8, 13, 13, TP, TP, REP),
            pltpu.SemaphoreType.DMA((11,)),
            pltpu.SemaphoreType.DMA((12,)),
        ],
        compiler_params=pltpu.CompilerParams(
            collective_id=0, has_side_effects=True, vmem_limit_bytes=60 << 20
        ),
        name="step",
    )(
        batch_rows, token_slots.reshape(TOK, 1), holder_map, holder_map, copies, upstream, up_act,
        master, moment1, moment2,
    )
    copy_next = jnp.concatenate([full.reshape(D, WIDE), adopted.reshape(D, UNIT)], axis=1)
    copy_next = jnp.where(own_entry == -2, jnp.zeros_like(copy_next), copy_next)
    return master_next, one_next, two_next, copy_next


def solution(mesh):
    placed = (
        P(("rep", "tp"), None),
        P("rep", None),
        P("rep", None),
        P("rep", "tp"),
        P("rep", "tp"),
        P("rep", "tp"),
        P("rep", "tp"),
        P("rep", "tp"),
        P("rep", "tp"),
    )
    return jax.shard_map(
        on_device,
        mesh=mesh,
        in_specs=placed,
        out_specs=(P("rep", "tp"), P("rep", "tp"), P("rep", "tp"), P("rep", "tp")),
        check_vma=False,
    )
```

```python
import functools
import math

import jax
import jax.numpy as jnp
from jax import lax
from jax.experimental import pallas as pl
from jax.experimental.pallas import tpu as pltpu
from jax.sharding import PartitionSpec as P

beta_one = 0.9
beta_two = 0.95
bias_one = 1.0 - 0.9**10
bias_two = 1.0 - 0.95**10
learn_rate = 0.05
weight_decay = 0.1
epsilon = 1e-08

D, TOK, WIDE, UNIT, NARROW = 4096, 384, 896, 128, 1024
REP, TP = 8, 16
OWN, SHARE = 96, 256
ROWS = D // REP
STRIP = ROWS // TP
SEVEN = WIDE // UNIT
PART = TOK // (TP // 2)
KINDS = REP // 2
LIMIT = 50
SCALING = 1.0 / math.sqrt(D)
MESH = pl.DeviceIdType.MESH
F32, BF16 = jnp.float32, jnp.bfloat16


class Place:
    def __init__(self):
        r, t = lax.axis_index("rep"), lax.axis_index("tp")
        self.r, self.t = r, t
        x, zl = r % 4, r // 4
        y, zh, c = t // 4, (t // 2) % 2, t % 2
        self.core = c
        self.chip = t // 2
        self.sibling = (r, t + 1 - 2 * c)

        def rep_id(step, flip):
            return (x + step) % 4 + 4 * ((zl + flip) % 2)

        def tp_id(step, flip):
            return ((y + step) % 4) * 4 + ((zh + flip) % 2) * 2 + c

        self.rep_ids = [[rep_id(s, f) for s in (0, 1, 3, 2)] for f in (0, 1)]
        self.tp_ids = [[tp_id(s, f) for s in (0, 1, 3, 2)] for f in (0, 1)]

    def rep_dev(self, other):
        return (other, self.t)

    def tp_dev(self, other):
        return (self.r, other)


def greet(place):
    barrier = pltpu.get_barrier_semaphore()

    def rep_mate(k, carry):
        pl.semaphore_signal(barrier, inc=1, device_id=((place.r + k) % REP, place.t), device_id_type=MESH)
        return carry

    def tp_mate(k, carry):
        pl.semaphore_signal(barrier, inc=1, device_id=(place.r, (place.t + k) % TP), device_id_type=MESH)
        return carry

    lax.fori_loop(1, REP, rep_mate, 0)
    lax.fori_loop(1, TP, tp_mate, 0)
    pl.semaphore_wait(barrier, REP + TP - 2)


class Tree:
    def __init__(self, view, ids, dev, ssem, rsem, extent, first):
        (me, nx, pv, op), (me_p, nx_p, pv_p, op_p) = ids
        to_nx, to_pv, to_pair = dev(nx), dev(pv), dev(me_p)
        half, a_half, rest = extent // 2, first // 2, extent - first
        self.rest, self.names = rest, dict(me=me, nx=nx, pv=pv, op=op, me_p=me_p, nx_p=nx_p, pv_p=pv_p, op_p=op_p)
        sent = {
            1: (me, 0, extent, to_nx), 2: (me, 0, extent, to_pv), 3: (me, 0, first, to_pair), 4: (me, first, rest, to_pair),
            5: (me_p, 0, first, to_nx), 6: (me_p, 0, first, to_pv), 7: (pv, 0, half, to_nx), 8: (nx, half, half, to_pv),
            9: (pv_p, 0, a_half, to_nx), 10: (nx_p, a_half, a_half, to_pv),
            11: (pv, first, rest, to_pair), 12: (nx, first, rest, to_pair), 13: (op, first, rest, to_pair),
        }
        got = {1: pv, 2: nx, 3: me_p, 4: me_p, 5: pv_p, 6: nx_p, 7: op, 8: op, 9: op_p, 10: op_p, 11: pv_p, 12: nx_p, 13: op_p}
        skipped = () if rest else (4, 11, 12, 13)
        self.out, self.into = {}, {}
        for i, (chunk, low, count, to) in sent.items():
            if i not in skipped:
                for book, which in ((self.out, chunk), (self.into, got[i])):
                    ref = view(which, low, count)
                    book[i] = pltpu.make_async_remote_copy(
                        src_ref=ref, dst_ref=ref, send_sem=ssem.at[i - 1], recv_sem=rsem.at[i - 1],
                        device_id=to, device_id_type=MESH,
                    )

    def start(self, *which):
        for i in which:
            if i in self.out:
                self.out[i].start()

    def wait(self, *which):
        for i in which:
            if i in self.into:
                self.into[i].wait_recv()

    def steps(self, done):
        def pair():
            self.wait(3)
            self.start(5, 6)
            if not self.rest:
                done("me_p")

        def previous():
            self.wait(1)
            self.start(7, 11)
            done("pv")

        def following():
            self.wait(2)
            self.start(8, 12)
            done("nx")

        def pair_previous():
            self.wait(5)
            self.start(9)
            if not self.rest:
                done("pv_p")

        def pair_following():
            self.wait(6)
            self.start(10)
            if not self.rest:
                done("nx_p")

        def opposite():
            self.wait(7, 8)
            self.start(13)
            done("op")

        def rests():
            if self.rest:
                self.wait(4)
                done("me_p")
                self.wait(11)
                done("pv_p")
                self.wait(12)
                done("nx_p")

        def last():
            self.wait(9, 10, 13)
            done("op_p")

        return [pair, previous, following, pair_previous, pair_following, opposite, rests, last]

    def begin(self):
        self.start(3, 1, 2, 4)

    def drain(self):
        for copy in self.out.values():
            copy.wait_send()


ORDER = ("me", "pv", "nx", "me_p", "op", "pv_p", "nx_p", "op_p")


class Siblings:
    def __init__(self, tree, view, extent, place, ssem, rsem):
        self.out, self.into = {}, {}
        for n, name in enumerate(ORDER):
            mine = tree.names[name]
            for book, which in ((self.out, mine), (self.into, mine + 1 - 2 * place.core)):
                ref = view(which, 0, extent)
                book[name] = pltpu.make_async_remote_copy(
                    src_ref=ref, dst_ref=ref, send_sem=ssem.at[n], recv_sem=rsem.at[n],
                    device_id=place.sibling, device_id_type=MESH,
                )

    def start(self, name):
        self.out[name].start()

    def wait(self, name):
        self.into[name].wait_recv()

    def drain(self):
        for copy in self.out.values():
            copy.wait_send()


def step_kernel(
    rows_ref, slots_ref, holders_ref, map_ref, copies_ref, upstream_ref, act_ref, master_ref, one_ref, two_ref,
    master, one, two, fresh, adopted, maps_out,
    own_rows, spread, inputs, column, choice, weight, gates, upstream, act, grad, pieces,
    parts, grads, total, strips, strewn, picked, routed, outgoing, maps,
    map_s, map_r, row_s, row_r, tree_s, tree_r, sib_s, sib_r, tree2_s, tree2_r, sib2_s, sib2_r,
    swap_s, swap_r, part_s, part_r, sib3_s, sib3_r, grad_s, grad_r, fresh_s, fresh_r,
    p1_s, p1_r, p2_s, p2_r, p3_s, p3_r, local,
):
    place = Place()
    r, t = place.r, place.t

    def loading(n, source, target):
        copy = pltpu.make_async_copy(source, target, local.at[n])
        copy.start()
        return copy

    load_rows = loading(0, rows_ref, own_rows)
    load_weight = loading(1, copies_ref, weight)
    load_factors = [loading(2, upstream_ref, upstream), loading(3, act_ref, act)]
    load_state = [loading(4, master_ref, master), loading(5, one_ref, one), loading(6, two_ref, two)]
    own_map = loading(7, map_ref, maps_out.at[r])
    greet(place)
    load_rows.wait()

    def each(count, act_on):
        lax.fori_loop(1, count, lambda k, c: (act_on(k), c)[1], 0)

    def remote(source, target, s, r_, k, to):
        return pltpu.make_async_remote_copy(
            src_ref=source, dst_ref=target, send_sem=s.at[k], recv_sem=r_.at[k], device_id=to, device_id_type=MESH
        )

    def columns_of(device):
        return pl.ds(pl.multiple_of(device * SHARE, SHARE), SHARE)

    def share_to(k):
        to = (t + k) % TP
        return remote(
            own_rows.at[:, pl.ds(pl.multiple_of(to * SHARE, SHARE), SHARE)],
            spread.at[pl.ds(pl.multiple_of(t * OWN, OWN), OWN), :], row_s, row_r, k, (r, to),
        )

    def share_from(k):
        source = (t + TP - k) % TP
        ref = spread.at[pl.ds(pl.multiple_of(source * OWN, OWN), OWN), :]
        return remote(ref, ref, row_s, row_r, k, (r, source))

    each(TP, lambda k: share_to(k).start())
    own_share = loading(
        8, own_rows.at[:, pl.ds(pl.multiple_of(t * SHARE, SHARE), SHARE)],
        spread.at[pl.ds(pl.multiple_of(t * OWN, OWN), OWN), :],
    )

    def map_to(k):
        return remote(map_ref, maps_out.at[r], map_s, map_r, k, ((r + k) % REP, t))

    def map_from(k):
        source = (r + REP - k) % REP
        return remote(map_ref, maps_out.at[source], map_s, map_r, k, (source, t))

    each(REP, lambda k: map_to(k).start())
    column[...] = jnp.broadcast_to(slots_ref[...], (128, TOK)).T

    def choose(n, carry):
        at = pl.ds(pl.multiple_of(n * 16, 16), 16)
        places = lax.broadcasted_iota(jnp.int32, (16, TP * OWN), 1)
        choice[at, :] = jnp.where(column[at, :1] == places, 1.0, 0.0).astype(BF16)
        return carry

    lax.fori_loop(0, TOK // 16, choose, 0)
    own_share.wait()
    each(TP, lambda k: share_from(k).wait_recv())

    inputs[:, columns_of(t)] = jnp.dot(choice[...], spread[...], preferred_element_type=F32).astype(BF16)

    def input_view(chunk, low, count):
        return inputs.at[pl.ds(low, count), columns_of(chunk)]

    tree = Tree(input_view, place.tp_ids, place.tp_dev, tree_s, tree_r, TOK, 224)
    sibs = Siblings(tree, input_view, TOK, place, sib_s, sib_r)
    tree.begin()
    sibs.start("me")
    load_weight.wait()

    def multiplied(name, first=False):
        sibs.wait(name)
        depth = pl.ds(pl.multiple_of(tree.names[name] // 2 * (2 * SHARE), 2 * SHARE), 2 * SHARE)
        for n in range(2):
            cols = slice(n * 512, (n + 1) * 512)
            part = jnp.dot(inputs[:, depth], weight[depth, cols], preferred_element_type=F32)
            gates[:, cols] = part if first else gates[:, cols] + part

    waiting = ["me"]

    def whole(name):
        sibs.start(name)
        waiting.append(name)
        if len(waiting) > 2:
            before = waiting.pop(0)
            multiplied(before, before == "me")

    for step in tree.steps(whole):
        step()
    for name in waiting:
        multiplied(name)

    mine_rows = pl.ds(pl.multiple_of(place.chip * PART, PART), PART)
    mine_cols = pl.ds(pl.multiple_of(place.core * SHARE, SHARE), SHARE)

    def swap_to(k):
        to = (r + k) % REP
        return remote(
            inputs.at[mine_rows, columns_of(2 * to + place.core)], parts.at[r, mine_rows, mine_cols], swap_s, swap_r, k, (to, t)
        )

    def swap_from(k):
        source = (r + REP - k) % REP
        ref = parts.at[source, mine_rows, mine_cols]
        return remote(ref, ref, swap_s, swap_r, k, (source, t))

    each(REP, lambda k: swap_to(k).start())
    own_swap = loading(9, inputs.at[mine_rows, columns_of(2 * r + place.core)], parts.at[r, mine_rows, mine_cols])

    for load in load_factors:
        load.wait()

    def gate_rows(tall, cols, keep):
        def rows(n, carry):
            at = pl.ds(pl.multiple_of(n * tall, tall), tall)
            gate = gates[at, cols] * SCALING
            logistic = 1.0 / (1.0 + jnp.exp(-gate))
            factors = upstream[at, cols].astype(F32) * act[at, cols].astype(F32)
            keep(at, (factors * logistic * (1.0 + gate * (1.0 - logistic))).astype(BF16))
            return carry

        lax.fori_loop(0, TOK // tall, rows, 0)

    def keep_piece(at, value):
        pieces[t, at, :] = value

    def keep_wide(at, value):
        grad[at, :] = value

    gate_rows(64, slice(WIDE, NARROW), keep_piece)

    def piece_view(chunk, low, count):
        return pieces.at[chunk, pl.ds(low, count), :]

    tree2 = Tree(piece_view, place.tp_ids, place.tp_dev, tree2_s, tree2_r, TOK, TOK)
    sibs2 = Siblings(tree2, piece_view, TOK, place, sib2_s, sib2_r)
    tree2.begin()
    sibs2.start("me")
    gate_rows(16, slice(0, WIDE), keep_wide)

    def part_view(chunk, low, count):
        at, side = chunk // 2, chunk % 2
        return parts.at[
            pl.ds(low, count),
            pl.ds(pl.multiple_of(at * PART, PART), PART),
            pl.ds(pl.multiple_of(side * SHARE, SHARE), SHARE),
        ]

    ptree = Tree(part_view, place.tp_ids, place.tp_dev, part_s, part_r, REP, REP)
    sibs3 = Siblings(ptree, part_view, REP, place, sib3_s, sib3_r)
    steps2 = tree2.steps(sibs2.start)
    for step in steps2[:5]:
        step()
    own_swap.wait()
    each(REP, lambda k: swap_from(k).wait_recv())
    ptree.begin()
    sibs3.start("me")
    for step in steps2[5:]:
        step()
    for name in ORDER:
        sibs2.wait(name)

    own_entry = holders_ref[0, t]
    for s in range(SEVEN):
        wanted = t * SEVEN + s
        owner = jnp.int32(0)
        for other in range(TP):
            owner = jnp.where(holders_ref[0, other] == wanted, other, owner)
        cols = slice(s * UNIT, (s + 1) * UNIT)
        grads[r, :, cols] = jnp.where(own_entry == -2, pieces[owner], grad[:, cols])

    def grad_view(chunk, low, count):
        return grads.at[chunk, pl.ds(low, count), :]

    gtree = Tree(grad_view, place.rep_ids, place.rep_dev, grad_s, grad_r, TOK, 256)
    gtree.begin()

    def gathered(chunk, first=False):
        part = lax.dot_general(
            parts[chunk], grads[chunk], (((0,), (0,)), ((), ())), preferred_element_type=F32
        )
        total[...] = part if first else total[...] + part

    own_map.wait()
    each(REP, lambda k: map_from(k).wait_recv())
    load_maps = loading(10, maps_out, maps)
    gsteps = gtree.steps(lambda name: gathered(gtree.names[name]))
    for step in ptree.steps(sibs3.start):
        step()
    gsteps[0]()
    for name in ORDER:
        sibs3.wait(name)
    gathered(r, True)
    for step in gsteps[1:]:
        step()

    for load in load_state:
        load.wait()

    def strip_of(device):
        return pl.ds(pl.multiple_of(device * STRIP, STRIP), STRIP)

    def one_to(k):
        to = (t + k) % TP
        return remote(strips.at[:, strip_of(to), :], strewn.at[pl.ds(t * SEVEN, SEVEN)], p1_s, p1_r, k, (r, to))

    def adam_rows(n, carry):
        at = pl.ds(pl.multiple_of(n * 16, 16), 16)
        gradient = total[at, :] * SCALING
        first_new = beta_one * one[at, :].astype(F32) + (1.0 - beta_one) * gradient
        second_new = beta_two * two[at, :].astype(F32) + (1.0 - beta_two) * gradient * gradient
        step_size = first_new / bias_one / (jnp.sqrt(second_new / bias_two) + epsilon)
        old = master[at, :]
        new = old - learn_rate * (step_size + weight_decay * old)
        master[at, :] = new
        one[at, :] = first_new.astype(BF16)
        two[at, :] = second_new.astype(BF16)
        low = new.astype(BF16)
        fresh[r, at, :] = low
        for s in range(SEVEN):
            strips[s, at, :] = low[:, s * UNIT : (s + 1) * UNIT]
        return carry

    def strip_done(k, carry):
        to = (t + 1 + k) % TP
        lax.fori_loop(2 * to, 2 * to + 2, adam_rows, 0)

        @pl.when(k < TP - 1)
        def _():
            one_to(k + 1).start()

        return carry

    lax.fori_loop(0, TP, strip_done, 0)

    def fresh_view(chunk, low, count):
        return fresh.at[chunk, pl.ds(low, count), :]

    ftree = Tree(fresh_view, place.rep_ids, place.rep_dev, fresh_s, fresh_r, ROWS, 320)

    def one_from(k):
        source = (t + TP - k) % TP
        ref = strewn.at[pl.ds(source * SEVEN, SEVEN)]
        return remote(ref, ref, p1_s, p1_r, k, (r, source))

    ftree.begin()
    strewn[pl.ds(t * SEVEN, SEVEN)] = strips[:, strip_of(t), :]

    load_maps.wait()
    narrow, rank, count = [], [], jnp.int32(0)
    for q in range(REP):
        narrow.append(maps[q, 0, 0] != -1)
        rank.append(jnp.minimum(count, KINDS - 1))
        count = count + jnp.where(narrow[q], 1, 0)
    which = []
    for k in range(KINDS):
        chosen = jnp.int32(0)
        for q in range(REP):
            chosen = jnp.where(narrow[q] & (rank[q] == k), q, chosen)
        which.append(chosen)

    each(TP, lambda k: one_from(k).wait_recv())
    for k in range(KINDS):

        def pick(to, carry, k=k):
            piece = maps[which[k], 0, to]
            value = strewn[jnp.maximum(piece, 0)]
            picked[to, k] = jnp.where(piece >= 0, value, jnp.zeros_like(value))
            return carry

        lax.fori_loop(0, TP, pick, 0)

    def two_to(k):
        to = (t + k) % TP
        return remote(picked.at[to], routed.at[:, strip_of(t), :], p2_s, p2_r, k, (r, to))

    def two_from(k):
        source = (t + TP - k) % TP
        ref = routed.at[:, strip_of(source), :]
        return remote(ref, ref, p2_s, p2_r, k, (r, source))

    each(TP, lambda k: two_to(k).start())
    routed[:, strip_of(t), :] = picked[t]

    fsteps = ftree.steps(lambda name: None)
    for step in fsteps[:3]:
        step()
    each(TP, lambda k: two_from(k).wait_recv())
    for q in range(REP):
        value = routed[rank[q]]
        outgoing[q] = jnp.where(narrow[q], value, jnp.zeros_like(value))

    def three_to(k):
        to = (r + k) % REP
        return remote(outgoing.at[to], adopted.at[r], p3_s, p3_r, k, (to, t))

    def three_from(k):
        source = (r + REP - k) % REP
        return remote(adopted.at[source], adopted.at[source], p3_s, p3_r, k, (source, t))

    each(REP, lambda k: three_to(k).start())
    adopted[r] = outgoing[r]
    for step in fsteps[3:]:
        step()
    each(REP, lambda k: three_from(k).wait_recv())

    for book in (tree, sibs, tree2, sibs2, ptree, sibs3, gtree, ftree):
        book.drain()
    each(REP, lambda k: map_to(k).wait_send())
    each(TP, lambda k: share_to(k).wait_send())
    each(REP, lambda k: swap_to(k).wait_send())
    each(TP, lambda k: one_to(k).wait_send())
    each(TP, lambda k: two_to(k).wait_send())
    each(REP, lambda k: three_to(k).wait_send())


def finish_kernel(
    holders_ref, master, one, two, fresh, adopted, master_out, one_out, two_out, copy_out, stage, outs
):
    failed = holders_ref[0, lax.axis_index("tp")] == -2
    stores = []

    def storing(source, target):
        copy = pltpu.make_async_copy(source, target, outs.at[len(stores)])
        copy.start()
        stores.append(copy)

    storing(master, master_out)
    storing(one, one_out)
    storing(two, two_out)
    for chunk in range(REP):

        def rows(n, carry, chunk=chunk):
            at = pl.ds(pl.multiple_of(n * 32, 32), 32)
            to = pl.ds(pl.multiple_of(chunk * ROWS + n * 32, 32), 32)
            for source, cols in ((fresh, slice(0, WIDE)), (adopted, slice(WIDE, NARROW))):
                value = source[chunk, at, :]
                stage[to, cols] = jnp.where(failed, jnp.zeros_like(value), value)
            return carry

        lax.fori_loop(0, ROWS // 32, rows, 0)
        span = pl.ds(chunk * ROWS, ROWS)
        storing(stage.at[span], copy_out.at[span])
    for store in stores:
        store.wait()


ANY = pl.BlockSpec(memory_space=pl.ANY)
VM = pl.BlockSpec(memory_space=pltpu.VMEM)
SM = pl.BlockSpec(memory_space=pltpu.SMEM)


def sems(*counts):
    return [pltpu.SemaphoreType.DMA((n,)) for n in counts for _ in (0, 1)]


def on_device(
    batch_rows, token_slots, holder_map, copies, upstream, up_act, master, moment1, moment2
):
    state = (
        jax.ShapeDtypeStruct((ROWS, WIDE), F32),
        jax.ShapeDtypeStruct((ROWS, WIDE), BF16),
        jax.ShapeDtypeStruct((ROWS, WIDE), BF16),
    )
    *held, _ = pl.pallas_call(
        step_kernel,
        out_shape=(
            *(pltpu.VMEM(a.shape, a.dtype) for a in state),
            pltpu.VMEM((REP, ROWS, WIDE), BF16),
            pltpu.VMEM((REP, ROWS, UNIT), BF16),
            jax.ShapeDtypeStruct((REP, 1, TP), jnp.int32),
        ),
        in_specs=[ANY, VM, SM, ANY, ANY, ANY, ANY, ANY, ANY, ANY],
        out_specs=(VM, VM, VM, VM, VM, ANY),
        scratch_shapes=[
            pltpu.VMEM((OWN, D), BF16),
            pltpu.VMEM((TP * OWN, SHARE), BF16),
            pltpu.VMEM((TOK, D), BF16),
            pltpu.VMEM((TOK, 128), jnp.int32),
            pltpu.VMEM((TOK, TP * OWN), BF16),
            pltpu.VMEM((D, NARROW), BF16),
            pltpu.VMEM((TOK, NARROW), F32),
            pltpu.VMEM((TOK, NARROW), BF16),
            pltpu.VMEM((TOK, NARROW), BF16),
            pltpu.VMEM((TOK, WIDE), BF16),
            pltpu.VMEM((TP, TOK, UNIT), BF16),
            pltpu.VMEM((REP, TOK, ROWS), BF16),
            pltpu.VMEM((REP, TOK, WIDE), BF16),
            pltpu.VMEM((ROWS, WIDE), F32),
            pltpu.VMEM((SEVEN, ROWS, UNIT), BF16),
            pltpu.VMEM((TP * SEVEN, STRIP, UNIT), BF16),
            pltpu.VMEM((TP, KINDS, STRIP, UNIT), BF16),
            pltpu.VMEM((KINDS, ROWS, UNIT), BF16),
            pltpu.VMEM((REP, ROWS, UNIT), BF16),
            pltpu.SMEM((REP, 1, TP), jnp.int32),
            *sems(REP, TP, 13, 8, 13, 8),
            *sems(REP, 13, 8, 13, 13, TP, TP, REP),
            pltpu.SemaphoreType.DMA((11,)),
        ],
        compiler_params=pltpu.CompilerParams(
            collective_id=0, has_side_effects=True, vmem_limit_bytes=LIMIT << 20
        ),
        name="step",
    )(
        batch_rows, token_slots, holder_map, holder_map, copies, upstream, up_act,
        master, moment1, moment2,
    )
    return pl.pallas_call(
        finish_kernel,
        out_shape=(*state, jax.ShapeDtypeStruct((D, NARROW), BF16)),
        in_specs=[SM, VM, VM, VM, VM, VM],
        out_specs=(ANY,) * 4,
        scratch_shapes=[pltpu.VMEM((D, NARROW), BF16), pltpu.SemaphoreType.DMA((11,))],
        compiler_params=pltpu.CompilerParams(vmem_limit_bytes=16 << 20),
        name="finish",
    )(holder_map, *held)


def solution(mesh):
    placed = (
        P(("rep", "tp"), None),
        P("rep", None),
        P("rep", None),
        P("rep", "tp"),
        P("rep", "tp"),
        P("rep", "tp"),
        P("rep", "tp"),
        P("rep", "tp"),
        P("rep", "tp"),
    )
    return jax.shard_map(
        on_device,
        mesh=mesh,
        in_specs=placed,
        out_specs=(P("rep", "tp"), P("rep", "tp"), P("rep", "tp"), P("rep", "tp")),
        check_vma=False,
    )
```

```python
import functools
import math

import jax
import jax.numpy as jnp
from jax import lax
from jax.experimental import pallas as pl
from jax.experimental.pallas import tpu as pltpu
from jax.sharding import PartitionSpec as P

beta_one = 0.9
beta_two = 0.95
bias_one = 1.0 - 0.9**10
bias_two = 1.0 - 0.95**10
learn_rate = 0.05
weight_decay = 0.1
epsilon = 1e-08

D, TOK, WIDE, UNIT, NARROW = 4096, 384, 896, 128, 1024
REP, TP = 8, 16
OWN, SHARE = 96, 256
ROWS = D // REP
STRIP = ROWS // TP
SEVEN = WIDE // UNIT
PART = TOK // (TP // 2)
KINDS = REP // 2
LIMIT = 50
HALF = TOK // 2
SCALING = 1.0 / math.sqrt(D)
MESH = pl.DeviceIdType.MESH
F32, BF16 = jnp.float32, jnp.bfloat16


class Place:
    def __init__(self):
        r, t = lax.axis_index("rep"), lax.axis_index("tp")
        self.r, self.t = r, t
        x, zl = r % 4, r // 4
        y, zh, c = t // 4, (t // 2) % 2, t % 2
        self.core = c
        self.chip = t // 2
        self.sibling = (r, t + 1 - 2 * c)

        def rep_id(step, flip):
            return (x + step) % 4 + 4 * ((zl + flip) % 2)

        def tp_id(step, flip):
            return ((y + step) % 4) * 4 + ((zh + flip) % 2) * 2 + c

        self.rep_ids = [[rep_id(s, f) for s in (0, 1, 3, 2)] for f in (0, 1)]
        self.tp_ids = [[tp_id(s, f) for s in (0, 1, 3, 2)] for f in (0, 1)]

    def rep_dev(self, other):
        return (other, self.t)

    def tp_dev(self, other):
        return (self.r, other)


def greet(place):
    barrier = pltpu.get_barrier_semaphore()

    def rep_mate(k, carry):
        pl.semaphore_signal(barrier, inc=1, device_id=((place.r + k) % REP, place.t), device_id_type=MESH)
        return carry

    def tp_mate(k, carry):
        pl.semaphore_signal(barrier, inc=1, device_id=(place.r, (place.t + k) % TP), device_id_type=MESH)
        return carry

    lax.fori_loop(1, REP, rep_mate, 0)
    lax.fori_loop(1, TP, tp_mate, 0)
    pl.semaphore_wait(barrier, REP + TP - 2)


class Tree:
    def __init__(self, view, ids, dev, ssem, rsem, extent, first, base=0):
        (me, nx, pv, op), (me_p, nx_p, pv_p, op_p) = ids
        to_nx, to_pv, to_pair = dev(nx), dev(pv), dev(me_p)
        half, a_half, rest = extent // 2, first // 2, extent - first
        self.rest, self.names = rest, dict(me=me, nx=nx, pv=pv, op=op, me_p=me_p, nx_p=nx_p, pv_p=pv_p, op_p=op_p)
        sent = {
            1: (me, 0, extent, to_nx), 2: (me, 0, extent, to_pv), 3: (me, 0, first, to_pair), 4: (me, first, rest, to_pair),
            5: (me_p, 0, first, to_nx), 6: (me_p, 0, first, to_pv), 7: (pv, 0, half, to_nx), 8: (nx, half, half, to_pv),
            9: (pv_p, 0, a_half, to_nx), 10: (nx_p, a_half, a_half, to_pv),
            11: (pv, first, rest, to_pair), 12: (nx, first, rest, to_pair), 13: (op, first, rest, to_pair),
        }
        got = {1: pv, 2: nx, 3: me_p, 4: me_p, 5: pv_p, 6: nx_p, 7: op, 8: op, 9: op_p, 10: op_p, 11: pv_p, 12: nx_p, 13: op_p}
        skipped = () if rest else (4, 11, 12, 13)
        self.out, self.into = {}, {}
        for i, (chunk, low, count, to) in sent.items():
            if i not in skipped:
                for book, which in ((self.out, chunk), (self.into, got[i])):
                    ref = view(which, low, count)
                    book[i] = pltpu.make_async_remote_copy(
                        src_ref=ref, dst_ref=ref, send_sem=ssem.at[base + i - 1], recv_sem=rsem.at[base + i - 1],
                        device_id=to, device_id_type=MESH,
                    )

    def start(self, *which):
        for i in which:
            if i in self.out:
                self.out[i].start()

    def wait(self, *which):
        for i in which:
            if i in self.into:
                self.into[i].wait_recv()

    def steps(self, done):
        def pair():
            self.wait(3)
            self.start(5, 6)
            if not self.rest:
                done("me_p")

        def previous():
            self.wait(1)
            self.start(7, 11)
            done("pv")

        def following():
            self.wait(2)
            self.start(8, 12)
            done("nx")

        def pair_previous():
            self.wait(5)
            self.start(9)
            if not self.rest:
                done("pv_p")

        def pair_following():
            self.wait(6)
            self.start(10)
            if not self.rest:
                done("nx_p")

        def opposite():
            self.wait(7, 8)
            self.start(13)
            done("op")

        def rests():
            if self.rest:
                self.wait(4)
                done("me_p")
                self.wait(11)
                done("pv_p")
                self.wait(12)
                done("nx_p")

        def last():
            self.wait(9, 10, 13)
            done("op_p")

        return [pair, previous, following, pair_previous, pair_following, opposite, rests, last]

    def begin(self):
        self.start(3, 1, 2, 4)

    def drain(self):
        for copy in self.out.values():
            copy.wait_send()


ORDER = ("me", "pv", "nx", "me_p", "op", "pv_p", "nx_p", "op_p")


class Siblings:
    def __init__(self, tree, view, extent, place, ssem, rsem, base=0):
        self.out, self.into = {}, {}
        for n, name in enumerate(ORDER):
            mine = tree.names[name]
            for book, which in ((self.out, mine), (self.into, mine + 1 - 2 * place.core)):
                ref = view(which, 0, extent)
                book[name] = pltpu.make_async_remote_copy(
                    src_ref=ref, dst_ref=ref, send_sem=ssem.at[base + n], recv_sem=rsem.at[base + n],
                    device_id=place.sibling, device_id_type=MESH,
                )

    def start(self, name):
        self.out[name].start()

    def wait(self, name):
        self.into[name].wait_recv()

    def drain(self):
        for copy in self.out.values():
            copy.wait_send()


def step_kernel(
    rows_ref, slots_ref, holders_ref, map_ref, copies_ref, upstream_ref, act_ref, master_ref, one_ref, two_ref,
    master, one, two, fresh, adopted, maps_out,
    own_rows, spread, inputs, column, choice, weight, gates, upstream, act, grad, early, later,
    parts, grads, total, strips, strewn, picked, routed, outgoing, maps,
    map_s, map_r, row_s, row_r, tree_s, tree_r, sib_s, sib_r, tree2_s, tree2_r, sib2_s, sib2_r,
    swap_s, swap_r, part_s, part_r, sib3_s, sib3_r, grad_s, grad_r, fresh_s, fresh_r,
    p1_s, p1_r, p2_s, p2_r, p3_s, p3_r, local,
):
    place = Place()
    r, t = place.r, place.t

    def loading(n, source, target):
        copy = pltpu.make_async_copy(source, target, local.at[n])
        copy.start()
        return copy

    load_rows = loading(0, rows_ref, own_rows)
    load_weight = loading(1, copies_ref, weight)
    load_factors = [loading(2, upstream_ref, upstream), loading(3, act_ref, act)]
    load_state = [loading(4, master_ref, master), loading(5, one_ref, one), loading(6, two_ref, two)]
    own_map = loading(7, map_ref, maps_out.at[r])
    greet(place)
    load_rows.wait()

    def each(count, act_on):
        lax.fori_loop(1, count, lambda k, c: (act_on(k), c)[1], 0)

    def remote(source, target, s, r_, k, to):
        return pltpu.make_async_remote_copy(
            src_ref=source, dst_ref=target, send_sem=s.at[k], recv_sem=r_.at[k], device_id=to, device_id_type=MESH
        )

    def columns_of(device):
        return pl.ds(pl.multiple_of(device * SHARE, SHARE), SHARE)

    def share_to(k):
        to = (t + k) % TP
        return remote(
            own_rows.at[:, pl.ds(pl.multiple_of(to * SHARE, SHARE), SHARE)],
            spread.at[pl.ds(pl.multiple_of(t * OWN, OWN), OWN), :], row_s, row_r, k, (r, to),
        )

    def share_from(k):
        source = (t + TP - k) % TP
        ref = spread.at[pl.ds(pl.multiple_of(source * OWN, OWN), OWN), :]
        return remote(ref, ref, row_s, row_r, k, (r, source))

    each(TP, lambda k: share_to(k).start())
    own_share = loading(
        8, own_rows.at[:, pl.ds(pl.multiple_of(t * SHARE, SHARE), SHARE)],
        spread.at[pl.ds(pl.multiple_of(t * OWN, OWN), OWN), :],
    )

    def map_to(k):
        return remote(map_ref, maps_out.at[r], map_s, map_r, k, ((r + k) % REP, t))

    def map_from(k):
        source = (r + REP - k) % REP
        return remote(map_ref, maps_out.at[source], map_s, map_r, k, (source, t))

    each(REP, lambda k: map_to(k).start())
    column[...] = jnp.broadcast_to(slots_ref[...], (128, TOK)).T

    def choose(n, carry):
        at = pl.ds(pl.multiple_of(n * 16, 16), 16)
        places = lax.broadcasted_iota(jnp.int32, (16, TP * OWN), 1)
        choice[at, :] = jnp.where(column[at, :1] == places, 1.0, 0.0).astype(BF16)
        return carry

    lax.fori_loop(0, TOK // 16, choose, 0)
    own_share.wait()
    each(TP, lambda k: share_from(k).wait_recv())

    inputs[:, columns_of(t)] = jnp.dot(choice[...], spread[...], preferred_element_type=F32).astype(BF16)

    def half_rows(half, low=0, count=HALF):
        return pl.ds(half * HALF + low, count)

    class Rows:
        def __init__(self, half):
            def view(chunk, low, count):
                return inputs.at[half_rows(half, low, count), columns_of(chunk)]

            self.half, self.waiting = half, ["me"]
            self.tree = Tree(view, place.tp_ids, place.tp_dev, tree_s, tree_r, HALF, 128, 13 * half)
            self.sibs = Siblings(self.tree, view, HALF, place, sib_s, sib_r, 8 * half)
            self.steps = self.tree.steps(self.whole)

        def begin(self):
            self.tree.begin()
            self.sibs.start("me")

        def multiplied(self):
            name = self.waiting.pop(0)
            self.sibs.wait(name)
            at = half_rows(self.half)
            depth = pl.ds(pl.multiple_of(self.tree.names[name] // 2 * (2 * SHARE), 2 * SHARE), 2 * SHARE)
            for n in range(2):
                cols = slice(n * 512, (n + 1) * 512)
                part = jnp.dot(inputs[at, depth], weight[depth, cols], preferred_element_type=F32)
                gates[at, cols] = part if name == "me" else gates[at, cols] + part

        def whole(self, name):
            self.sibs.start(name)
            self.waiting.append(name)
            if len(self.waiting) > 2:
                self.multiplied()

        def run(self, first, last):
            for step in self.steps[first:last]:
                step()

        def finish(self):
            while self.waiting:
                self.multiplied()

    def gate_rows(half, tall, cols, keep):
        def rows(n, carry):
            at = pl.ds(pl.multiple_of(half * HALF + n * tall, tall), tall)
            gate = gates[at, cols] * SCALING
            logistic = 1.0 / (1.0 + jnp.exp(-gate))
            factors = upstream[at, cols].astype(F32) * act[at, cols].astype(F32)
            keep(n * tall, (factors * logistic * (1.0 + gate * (1.0 - logistic))).astype(BF16))
            return carry

        lax.fori_loop(0, HALF // tall, rows, 0)

    own_entry = holders_ref[0, t]
    owners = []
    for s in range(SEVEN):
        owner = jnp.int32(0)
        for other in range(TP):
            owner = jnp.where(holders_ref[0, other] == t * SEVEN + s, other, owner)
        owners.append(owner)

    class Pieces:
        def __init__(self, half):
            buffer = later if half else early

            def view(chunk, low, count):
                return buffer.at[chunk, pl.ds(low, count), :]

            self.half, self.buffer = half, buffer
            self.tree = Tree(view, place.tp_ids, place.tp_dev, tree2_s, tree2_r, HALF, HALF, 13 * half)
            self.sibs = Siblings(self.tree, view, HALF, place, sib2_s, sib2_r, 8 * half)
            self.steps = self.tree.steps(self.sibs.start)

        def begin(self):
            def keep(low, value):
                self.buffer[t, pl.ds(pl.multiple_of(low, 64), 64), :] = value

            gate_rows(self.half, 64, slice(WIDE, NARROW), keep)
            self.tree.begin()
            self.sibs.start("me")

        def wide(self):
            def keep(low, value):
                grad[pl.ds(pl.multiple_of(self.half * HALF + low, 16), 16), :] = value

            gate_rows(self.half, 16, slice(0, WIDE), keep)

        def run(self, first, last):
            for step in self.steps[first:last]:
                step()

        def choose(self):
            for name in ORDER:
                self.sibs.wait(name)
            at = slice(self.half * HALF, (self.half + 1) * HALF)
            for s, owner in enumerate(owners):
                cols = slice(s * UNIT, (s + 1) * UNIT)
                grads[r, at, cols] = jnp.where(own_entry == -2, self.buffer[owner], grad[at, cols])

    def gathered(chunk, first=False):
        part = lax.dot_general(
            parts[chunk], grads[chunk], (((0,), (0,)), ((), ())), preferred_element_type=F32
        )
        total[...] = part if first else total[...] + part

    def grad_tree(half):
        def view(chunk, low, count):
            return grads.at[chunk, half_rows(half, low, count), :]

        return Tree(view, place.rep_ids, place.rep_dev, grad_s, grad_r, HALF, 128, 13 * half)

    rows_a, rows_b = Rows(0), Rows(1)
    pieces_a, pieces_b = Pieces(0), Pieces(1)
    gtree_a, gtree_b = grad_tree(0), grad_tree(1)

    rows_a.begin()
    load_weight.wait()
    rows_a.run(0, 3)
    rows_b.begin()
    rows_a.run(3, 8)
    rows_a.finish()
    for load in load_factors:
        load.wait()
    pieces_a.begin()
    rows_b.run(0, 3)
    pieces_a.wide()
    pieces_a.run(0, 1)
    rows_b.run(3, 5)
    pieces_a.run(1, 3)
    rows_b.run(5, 8)
    rows_b.finish()
    pieces_b.begin()
    pieces_a.run(3, 8)

    mine_rows = pl.ds(pl.multiple_of(place.chip * PART, PART), PART)
    mine_cols = pl.ds(pl.multiple_of(place.core * SHARE, SHARE), SHARE)

    def swap_to(k):
        to = (r + k) % REP
        return remote(
            inputs.at[mine_rows, columns_of(2 * to + place.core)], parts.at[r, mine_rows, mine_cols], swap_s, swap_r, k, (to, t)
        )

    def swap_from(k):
        source = (r + REP - k) % REP
        ref = parts.at[source, mine_rows, mine_cols]
        return remote(ref, ref, swap_s, swap_r, k, (source, t))

    each(REP, lambda k: swap_to(k).start())
    own_swap = loading(9, inputs.at[mine_rows, columns_of(2 * r + place.core)], parts.at[r, mine_rows, mine_cols])

    def part_view(chunk, low, count):
        at, side = chunk // 2, chunk % 2
        return parts.at[
            pl.ds(low, count),
            pl.ds(pl.multiple_of(at * PART, PART), PART),
            pl.ds(pl.multiple_of(side * SHARE, SHARE), SHARE),
        ]

    ptree = Tree(part_view, place.tp_ids, place.tp_dev, part_s, part_r, REP, REP)
    sibs3 = Siblings(ptree, part_view, REP, place, sib3_s, sib3_r)
    psteps = ptree.steps(sibs3.start)
    gsteps_a = gtree_a.steps(lambda name: None)
    late = []
    gsteps_b = gtree_b.steps(late.append)

    def run(*steps):
        for step in steps:
            step()

    pieces_a.choose()
    gtree_a.begin()
    pieces_b.wide()
    pieces_b.run(0, 3)
    own_swap.wait()
    each(REP, lambda k: swap_from(k).wait_recv())
    ptree.begin()
    sibs3.start("me")
    pieces_b.run(3, 8)
    run(*gsteps_a[:3])
    pieces_b.choose()
    gtree_b.begin()
    own_map.wait()
    each(REP, lambda k: map_from(k).wait_recv())
    load_maps = loading(10, maps_out, maps)
    run(*psteps[:3], *gsteps_a[3:5], *psteps[3:], gsteps_b[0], *gsteps_a[5:], *gsteps_b[1:3])
    for name in ORDER:
        sibs3.wait(name)
    gathered(r, True)
    for step in gsteps_b[3:]:
        while late:
            gathered(gtree_b.names[late.pop(0)])
        step()
    while late:
        gathered(gtree_b.names[late.pop(0)])

    for load in load_state:
        load.wait()

    def strip_of(device):
        return pl.ds(pl.multiple_of(device * STRIP, STRIP), STRIP)

    def one_to(k):
        to = (t + k) % TP
        return remote(strips.at[:, strip_of(to), :], strewn.at[pl.ds(t * SEVEN, SEVEN)], p1_s, p1_r, k, (r, to))

    def adam_rows(n, carry):
        at = pl.ds(pl.multiple_of(n * 16, 16), 16)
        gradient = total[at, :] * SCALING
        first_new = beta_one * one[at, :].astype(F32) + (1.0 - beta_one) * gradient
        second_new = beta_two * two[at, :].astype(F32) + (1.0 - beta_two) * gradient * gradient
        step_size = first_new / bias_one / (jnp.sqrt(second_new / bias_two) + epsilon)
        old = master[at, :]
        new = old - learn_rate * (step_size + weight_decay * old)
        master[at, :] = new
        one[at, :] = first_new.astype(BF16)
        two[at, :] = second_new.astype(BF16)
        low = new.astype(BF16)
        fresh[r, at, :] = low
        for s in range(SEVEN):
            strips[s, at, :] = low[:, s * UNIT : (s + 1) * UNIT]
        return carry

    def strip_done(k, carry):
        to = (t + 1 + k) % TP
        lax.fori_loop(2 * to, 2 * to + 2, adam_rows, 0)

        @pl.when(k < TP - 1)
        def _():
            one_to(k + 1).start()

        return carry

    lax.fori_loop(0, TP, strip_done, 0)

    def fresh_view(chunk, low, count):
        return fresh.at[chunk, pl.ds(low, count), :]

    ftree = Tree(fresh_view, place.rep_ids, place.rep_dev, fresh_s, fresh_r, ROWS, 320)

    def one_from(k):
        source = (t + TP - k) % TP
        ref = strewn.at[pl.ds(source * SEVEN, SEVEN)]
        return remote(ref, ref, p1_s, p1_r, k, (r, source))

    ftree.begin()
    strewn[pl.ds(t * SEVEN, SEVEN)] = strips[:, strip_of(t), :]

    load_maps.wait()
    narrow, rank, count = [], [], jnp.int32(0)
    for q in range(REP):
        narrow.append(maps[q, 0, 0] != -1)
        rank.append(jnp.minimum(count, KINDS - 1))
        count = count + jnp.where(narrow[q], 1, 0)
    which = []
    for k in range(KINDS):
        chosen = jnp.int32(0)
        for q in range(REP):
            chosen = jnp.where(narrow[q] & (rank[q] == k), q, chosen)
        which.append(chosen)

    each(TP, lambda k: one_from(k).wait_recv())
    for k in range(KINDS):

        def pick(to, carry, k=k):
            piece = maps[which[k], 0, to]
            value = strewn[jnp.maximum(piece, 0)]
            picked[to, k] = jnp.where(piece >= 0, value, jnp.zeros_like(value))
            return carry

        lax.fori_loop(0, TP, pick, 0)

    def two_to(k):
        to = (t + k) % TP
        return remote(picked.at[to], routed.at[:, strip_of(t), :], p2_s, p2_r, k, (r, to))

    def two_from(k):
        source = (t + TP - k) % TP
        ref = routed.at[:, strip_of(source), :]
        return remote(ref, ref, p2_s, p2_r, k, (r, source))

    each(TP, lambda k: two_to(k).start())
    routed[:, strip_of(t), :] = picked[t]

    fsteps = ftree.steps(lambda name: None)
    for step in fsteps[:3]:
        step()
    each(TP, lambda k: two_from(k).wait_recv())
    for q in range(REP):
        value = routed[rank[q]]
        outgoing[q] = jnp.where(narrow[q], value, jnp.zeros_like(value))

    def three_to(k):
        to = (r + k) % REP
        return remote(outgoing.at[to], adopted.at[r], p3_s, p3_r, k, (to, t))

    def three_from(k):
        source = (r + REP - k) % REP
        return remote(adopted.at[source], adopted.at[source], p3_s, p3_r, k, (source, t))

    each(REP, lambda k: three_to(k).start())
    adopted[r] = outgoing[r]
    for step in fsteps[3:]:
        step()
    each(REP, lambda k: three_from(k).wait_recv())

    for part in (rows_a, rows_b, pieces_a, pieces_b):
        part.tree.drain()
        part.sibs.drain()
    for book in (ptree, sibs3, gtree_a, gtree_b, ftree):
        book.drain()
    each(REP, lambda k: map_to(k).wait_send())
    each(TP, lambda k: share_to(k).wait_send())
    each(REP, lambda k: swap_to(k).wait_send())
    each(TP, lambda k: one_to(k).wait_send())
    each(TP, lambda k: two_to(k).wait_send())
    each(REP, lambda k: three_to(k).wait_send())


def finish_kernel(
    holders_ref, master, one, two, fresh, adopted, master_out, one_out, two_out, copy_out, stage, outs
):
    failed = holders_ref[0, lax.axis_index("tp")] == -2
    stores = []

    def storing(source, target):
        copy = pltpu.make_async_copy(source, target, outs.at[len(stores)])
        copy.start()
        stores.append(copy)

    storing(master, master_out)
    storing(one, one_out)
    storing(two, two_out)
    for chunk in range(REP):

        def rows(n, carry, chunk=chunk):
            at = pl.ds(pl.multiple_of(n * 32, 32), 32)
            to = pl.ds(pl.multiple_of(chunk * ROWS + n * 32, 32), 32)
            for source, cols in ((fresh, slice(0, WIDE)), (adopted, slice(WIDE, NARROW))):
                value = source[chunk, at, :]
                stage[to, cols] = jnp.where(failed, jnp.zeros_like(value), value)
            return carry

        lax.fori_loop(0, ROWS // 32, rows, 0)
        span = pl.ds(chunk * ROWS, ROWS)
        storing(stage.at[span], copy_out.at[span])
    for store in stores:
        store.wait()


ANY = pl.BlockSpec(memory_space=pl.ANY)
VM = pl.BlockSpec(memory_space=pltpu.VMEM)
SM = pl.BlockSpec(memory_space=pltpu.SMEM)


def sems(*counts):
    return [pltpu.SemaphoreType.DMA((n,)) for n in counts for _ in (0, 1)]


def on_device(
    batch_rows, token_slots, holder_map, copies, upstream, up_act, master, moment1, moment2
):
    state = (
        jax.ShapeDtypeStruct((ROWS, WIDE), F32),
        jax.ShapeDtypeStruct((ROWS, WIDE), BF16),
        jax.ShapeDtypeStruct((ROWS, WIDE), BF16),
    )
    *held, _ = pl.pallas_call(
        step_kernel,
        out_shape=(
            *(pltpu.VMEM(a.shape, a.dtype) for a in state),
            pltpu.VMEM((REP, ROWS, WIDE), BF16),
            pltpu.VMEM((REP, ROWS, UNIT), BF16),
            jax.ShapeDtypeStruct((REP, 1, TP), jnp.int32),
        ),
        in_specs=[ANY, VM, SM, ANY, ANY, ANY, ANY, ANY, ANY, ANY],
        out_specs=(VM, VM, VM, VM, VM, ANY),
        scratch_shapes=[
            pltpu.VMEM((OWN, D), BF16),
            pltpu.VMEM((TP * OWN, SHARE), BF16),
            pltpu.VMEM((TOK, D), BF16),
            pltpu.VMEM((TOK, 128), jnp.int32),
            pltpu.VMEM((TOK, TP * OWN), BF16),
            pltpu.VMEM((D, NARROW), BF16),
            pltpu.VMEM((TOK, NARROW), F32),
            pltpu.VMEM((TOK, NARROW), BF16),
            pltpu.VMEM((TOK, NARROW), BF16),
            pltpu.VMEM((TOK, WIDE), BF16),
            pltpu.VMEM((TP, HALF, UNIT), BF16),
            pltpu.VMEM((TP, HALF, UNIT), BF16),
            pltpu.VMEM((REP, TOK, ROWS), BF16),
            pltpu.VMEM((REP, TOK, WIDE), BF16),
            pltpu.VMEM((ROWS, WIDE), F32),
            pltpu.VMEM((SEVEN, ROWS, UNIT), BF16),
            pltpu.VMEM((TP * SEVEN, STRIP, UNIT), BF16),
            pltpu.VMEM((TP, KINDS, STRIP, UNIT), BF16),
            pltpu.VMEM((KINDS, ROWS, UNIT), BF16),
            pltpu.VMEM((REP, ROWS, UNIT), BF16),
            pltpu.SMEM((REP, 1, TP), jnp.int32),
            *sems(REP, TP, 26, 16, 26, 16),
            *sems(REP, 13, 8, 26, 13, TP, TP, REP),
            pltpu.SemaphoreType.DMA((11,)),
        ],
        compiler_params=pltpu.CompilerParams(
            collective_id=0, has_side_effects=True, vmem_limit_bytes=LIMIT << 20
        ),
        name="step",
    )(
        batch_rows, token_slots, holder_map, holder_map, copies, upstream, up_act,
        master, moment1, moment2,
    )
    return pl.pallas_call(
        finish_kernel,
        out_shape=(*state, jax.ShapeDtypeStruct((D, NARROW), BF16)),
        in_specs=[SM, VM, VM, VM, VM, VM],
        out_specs=(ANY,) * 4,
        scratch_shapes=[pltpu.VMEM((D, NARROW), BF16), pltpu.SemaphoreType.DMA((11,))],
        compiler_params=pltpu.CompilerParams(vmem_limit_bytes=16 << 20),
        name="finish",
    )(holder_map, *held)


def solution(mesh):
    placed = (
        P(("rep", "tp"), None),
        P("rep", None),
        P("rep", None),
        P("rep", "tp"),
        P("rep", "tp"),
        P("rep", "tp"),
        P("rep", "tp"),
        P("rep", "tp"),
        P("rep", "tp"),
    )
    return jax.shard_map(
        on_device,
        mesh=mesh,
        in_specs=placed,
        out_specs=(P("rep", "tp"), P("rep", "tp"), P("rep", "tp"), P("rep", "tp")),
        check_vma=False,
    )
```

```python
import functools
import math

import jax
import jax.numpy as jnp
from jax import lax
from jax.experimental import pallas as pl
from jax.experimental.pallas import tpu as pltpu
from jax.sharding import PartitionSpec as P

beta_one = 0.9
beta_two = 0.95
bias_one = 1.0 - 0.9**10
bias_two = 1.0 - 0.95**10
learn_rate = 0.05
weight_decay = 0.1
epsilon = 1e-08

D, TOK, WIDE, UNIT, NARROW = 4096, 384, 896, 128, 1024
REP, TP = 8, 16
OWN, SHARE = 96, 256
ROWS = D // REP
STRIP = ROWS // TP
SEVEN = WIDE // UNIT
PART = TOK // (TP // 2)
KINDS = REP // 2
LIMIT = 50
HALF = TOK // 2
SCALING = 1.0 / math.sqrt(D)
MESH = pl.DeviceIdType.MESH
F32, BF16 = jnp.float32, jnp.bfloat16


class Place:
    def __init__(self):
        r, t = lax.axis_index("rep"), lax.axis_index("tp")
        self.r, self.t = r, t
        x, zl = r % 4, r // 4
        y, zh, c = t // 4, (t // 2) % 2, t % 2
        self.core = c
        self.chip = t // 2
        self.sibling = (r, t + 1 - 2 * c)

        def rep_id(step, flip):
            return (x + step) % 4 + 4 * ((zl + flip) % 2)

        def tp_id(step, flip):
            return ((y + step) % 4) * 4 + ((zh + flip) % 2) * 2 + c

        self.rep_ids = [[rep_id(s, f) for s in (0, 1, 3, 2)] for f in (0, 1)]
        self.tp_ids = [[tp_id(s, f) for s in (0, 1, 3, 2)] for f in (0, 1)]

    def rep_dev(self, other):
        return (other, self.t)

    def tp_dev(self, other):
        return (self.r, other)


def greet(place):
    barrier = pltpu.get_barrier_semaphore()

    def rep_mate(k, carry):
        pl.semaphore_signal(barrier, inc=1, device_id=((place.r + k) % REP, place.t), device_id_type=MESH)
        return carry

    def tp_mate(k, carry):
        pl.semaphore_signal(barrier, inc=1, device_id=(place.r, (place.t + k) % TP), device_id_type=MESH)
        return carry

    lax.fori_loop(1, REP, rep_mate, 0)
    lax.fori_loop(1, TP, tp_mate, 0)
    pl.semaphore_wait(barrier, REP + TP - 2)


class Tree:
    def __init__(self, view, ids, dev, ssem, rsem, extent, first, base=0):
        (me, nx, pv, op), (me_p, nx_p, pv_p, op_p) = ids
        to_nx, to_pv, to_pair = dev(nx), dev(pv), dev(me_p)
        half, a_half, rest = extent // 2, first // 2, extent - first
        self.rest, self.names = rest, dict(me=me, nx=nx, pv=pv, op=op, me_p=me_p, nx_p=nx_p, pv_p=pv_p, op_p=op_p)
        sent = {
            1: (me, 0, extent, to_nx), 2: (me, 0, extent, to_pv), 3: (me, 0, first, to_pair), 4: (me, first, rest, to_pair),
            5: (me_p, 0, first, to_nx), 6: (me_p, 0, first, to_pv), 7: (pv, 0, half, to_nx), 8: (nx, half, half, to_pv),
            9: (pv_p, 0, a_half, to_nx), 10: (nx_p, a_half, a_half, to_pv),
            11: (pv, first, rest, to_pair), 12: (nx, first, rest, to_pair), 13: (op, first, rest, to_pair),
        }
        got = {1: pv, 2: nx, 3: me_p, 4: me_p, 5: pv_p, 6: nx_p, 7: op, 8: op, 9: op_p, 10: op_p, 11: pv_p, 12: nx_p, 13: op_p}
        skipped = () if rest else (4, 11, 12, 13)
        self.out, self.into = {}, {}
        for i, (chunk, low, count, to) in sent.items():
            if i not in skipped:
                for book, which in ((self.out, chunk), (self.into, got[i])):
                    ref = view(which, low, count)
                    book[i] = pltpu.make_async_remote_copy(
                        src_ref=ref, dst_ref=ref, send_sem=ssem.at[base + i - 1], recv_sem=rsem.at[base + i - 1],
                        device_id=to, device_id_type=MESH,
                    )

    def start(self, *which):
        for i in which:
            if i in self.out:
                self.out[i].start()

    def wait(self, *which):
        for i in which:
            if i in self.into:
                self.into[i].wait_recv()

    def steps(self, done):
        def pair():
            self.wait(3)
            self.start(5, 6)
            if not self.rest:
                done("me_p")

        def previous():
            self.wait(1)
            self.start(7, 11)
            done("pv")

        def following():
            self.wait(2)
            self.start(8, 12)
            done("nx")

        def pair_previous():
            self.wait(5)
            self.start(9)
            if not self.rest:
                done("pv_p")

        def pair_following():
            self.wait(6)
            self.start(10)
            if not self.rest:
                done("nx_p")

        def opposite():
            self.wait(7, 8)
            self.start(13)
            done("op")

        def rests():
            if self.rest:
                self.wait(4)
                done("me_p")
                self.wait(11)
                done("pv_p")
                self.wait(12)
                done("nx_p")

        def last():
            self.wait(9, 10, 13)
            done("op_p")

        return [pair, previous, following, pair_previous, pair_following, opposite, rests, last]

    def begin(self):
        self.start(3, 1, 2, 4)

    def drain(self):
        for copy in self.out.values():
            copy.wait_send()


ORDER = ("me", "pv", "nx", "me_p", "op", "pv_p", "nx_p", "op_p")


class Siblings:
    def __init__(self, tree, view, extent, place, ssem, rsem, base=0):
        self.out, self.into = {}, {}
        for n, name in enumerate(ORDER):
            mine = tree.names[name]
            for book, which in ((self.out, mine), (self.into, mine + 1 - 2 * place.core)):
                ref = view(which, 0, extent)
                book[name] = pltpu.make_async_remote_copy(
                    src_ref=ref, dst_ref=ref, send_sem=ssem.at[base + n], recv_sem=rsem.at[base + n],
                    device_id=place.sibling, device_id_type=MESH,
                )

    def start(self, name):
        self.out[name].start()

    def wait(self, name):
        self.into[name].wait_recv()

    def drain(self):
        for copy in self.out.values():
            copy.wait_send()


def step_kernel(
    rows_ref, slots_ref, holders_ref, map_ref, copies_ref, upstream_ref, act_ref, master_ref, one_ref, two_ref,
    master, one, two, fresh, adopted, maps_out,
    own_rows, spread, inputs, column, choice, weight, gates, upstream, act, grad, early, later,
    parts, grads, total, strips, strewn, picked, routed, outgoing, maps,
    map_s, map_r, row_s, row_r, tree_s, tree_r, sib_s, sib_r, tree2_s, tree2_r, sib2_s, sib2_r,
    swap_s, swap_r, part_s, part_r, sib3_s, sib3_r, grad_s, grad_r, fresh_s, fresh_r,
    p1_s, p1_r, p2_s, p2_r, p3_s, p3_r, local,
):
    place = Place()
    r, t = place.r, place.t

    def loading(n, source, target):
        copy = pltpu.make_async_copy(source, target, local.at[n])
        copy.start()
        return copy

    load_rows = loading(0, rows_ref, own_rows)
    load_weight = loading(1, copies_ref, weight)
    load_factors = [loading(2, upstream_ref, upstream), loading(3, act_ref, act)]
    load_state = [loading(4, master_ref, master), loading(5, one_ref, one), loading(6, two_ref, two)]
    own_map = loading(7, map_ref, maps_out.at[r])
    greet(place)
    load_rows.wait()

    def each(count, act_on):
        lax.fori_loop(1, count, lambda k, c: (act_on(k), c)[1], 0)

    def remote(source, target, s, r_, k, to):
        return pltpu.make_async_remote_copy(
            src_ref=source, dst_ref=target, send_sem=s.at[k], recv_sem=r_.at[k], device_id=to, device_id_type=MESH
        )

    def columns_of(device):
        return pl.ds(pl.multiple_of(device * SHARE, SHARE), SHARE)

    def share_to(k):
        to = (t + k) % TP
        return remote(
            own_rows.at[:, pl.ds(pl.multiple_of(to * SHARE, SHARE), SHARE)],
            spread.at[pl.ds(pl.multiple_of(t * OWN, OWN), OWN), :], row_s, row_r, k, (r, to),
        )

    def share_from(k):
        source = (t + TP - k) % TP
        ref = spread.at[pl.ds(pl.multiple_of(source * OWN, OWN), OWN), :]
        return remote(ref, ref, row_s, row_r, k, (r, source))

    each(TP, lambda k: share_to(k).start())
    own_share = loading(
        8, own_rows.at[:, pl.ds(pl.multiple_of(t * SHARE, SHARE), SHARE)],
        spread.at[pl.ds(pl.multiple_of(t * OWN, OWN), OWN), :],
    )

    def map_to(k):
        return remote(map_ref, maps_out.at[r], map_s, map_r, k, ((r + k) % REP, t))

    def map_from(k):
        source = (r + REP - k) % REP
        return remote(map_ref, maps_out.at[source], map_s, map_r, k, (source, t))

    each(REP, lambda k: map_to(k).start())
    column[...] = jnp.broadcast_to(slots_ref[...], (128, TOK)).T

    def choose(n, carry):
        at = pl.ds(pl.multiple_of(n * 16, 16), 16)
        places = lax.broadcasted_iota(jnp.int32, (16, TP * OWN), 1)
        choice[at, :] = jnp.where(column[at, :1] == places, 1.0, 0.0).astype(BF16)
        return carry

    lax.fori_loop(0, TOK // 16, choose, 0)
    own_share.wait()
    each(TP, lambda k: share_from(k).wait_recv())

    inputs[:, columns_of(t)] = jnp.dot(choice[...], spread[...], preferred_element_type=F32).astype(BF16)

    def half_rows(half, low=0, count=HALF):
        return pl.ds(half * HALF + low, count)

    class Rows:
        def __init__(self, half):
            def view(chunk, low, count):
                return inputs.at[half_rows(half, low, count), columns_of(chunk)]

            self.half, self.waiting = half, ["me"]
            self.tree = Tree(view, place.tp_ids, place.tp_dev, tree_s, tree_r, HALF, 128, 13 * half)
            self.sibs = Siblings(self.tree, view, HALF, place, sib_s, sib_r, 8 * half)
            self.steps = self.tree.steps(self.whole)

        def begin(self):
            self.tree.begin()
            self.sibs.start("me")

        def multiplied(self):
            name = self.waiting.pop(0)
            self.sibs.wait(name)
            at = half_rows(self.half)
            depth = pl.ds(pl.multiple_of(self.tree.names[name] // 2 * (2 * SHARE), 2 * SHARE), 2 * SHARE)
            for n in range(2):
                cols = slice(n * 512, (n + 1) * 512)
                part = jnp.dot(inputs[at, depth], weight[depth, cols], preferred_element_type=F32)
                gates[at, cols] = part if name == "me" else gates[at, cols] + part

        def whole(self, name):
            self.sibs.start(name)
            self.waiting.append(name)
            if len(self.waiting) > 2:
                self.multiplied()

        def run(self, first, last):
            for step in self.steps[first:last]:
                step()

        def finish(self):
            while self.waiting:
                self.multiplied()

    def gate_rows(half, tall, cols, keep):
        def rows(n, carry):
            at = pl.ds(pl.multiple_of(half * HALF + n * tall, tall), tall)
            gate = gates[at, cols] * SCALING
            logistic = 1.0 / (1.0 + jnp.exp(-gate))
            factors = upstream[at, cols].astype(F32) * act[at, cols].astype(F32)
            keep(n * tall, (factors * logistic * (1.0 + gate * (1.0 - logistic))).astype(BF16))
            return carry

        lax.fori_loop(0, HALF // tall, rows, 0)

    own_entry = holders_ref[0, t]
    owners = []
    for s in range(SEVEN):
        owner = jnp.int32(0)
        for other in range(TP):
            owner = jnp.where(holders_ref[0, other] == t * SEVEN + s, other, owner)
        owners.append(owner)

    class Pieces:
        def __init__(self, half):
            buffer = later if half else early

            def view(chunk, low, count):
                return buffer.at[chunk, pl.ds(low, count), :]

            self.half, self.buffer = half, buffer
            self.tree = Tree(view, place.tp_ids, place.tp_dev, tree2_s, tree2_r, HALF, HALF, 13 * half)
            self.sibs = Siblings(self.tree, view, HALF, place, sib2_s, sib2_r, 8 * half)
            self.steps = self.tree.steps(self.sibs.start)

        def begin(self):
            def keep(low, value):
                self.buffer[t, pl.ds(pl.multiple_of(low, 64), 64), :] = value

            gate_rows(self.half, 64, slice(WIDE, NARROW), keep)
            self.tree.begin()
            self.sibs.start("me")

        def wide(self):
            def keep(low, value):
                grad[pl.ds(pl.multiple_of(self.half * HALF + low, 16), 16), :] = value

            gate_rows(self.half, 16, slice(0, WIDE), keep)

        def run(self, first, last):
            for step in self.steps[first:last]:
                step()

        def choose(self):
            for name in ORDER:
                self.sibs.wait(name)
            at = slice(self.half * HALF, (self.half + 1) * HALF)
            for s, owner in enumerate(owners):
                cols = slice(s * UNIT, (s + 1) * UNIT)
                grads[r, at, cols] = jnp.where(own_entry == -2, self.buffer[owner], grad[at, cols])

    def gathered(chunk, first=False):
        part = lax.dot_general(
            parts[chunk], grads[chunk], (((0,), (0,)), ((), ())), preferred_element_type=F32
        )
        total[...] = part if first else total[...] + part

    def grad_tree(half):
        def view(chunk, low, count):
            return grads.at[chunk, half_rows(half, low, count), :]

        return Tree(view, place.rep_ids, place.rep_dev, grad_s, grad_r, HALF, 128, 13 * half)

    rows_a, rows_b = Rows(0), Rows(1)
    pieces_a, pieces_b = Pieces(0), Pieces(1)
    gtree_a, gtree_b = grad_tree(0), grad_tree(1)

    rows_a.begin()
    load_weight.wait()
    rows_a.run(0, 3)
    rows_b.begin()
    rows_a.run(3, 8)
    rows_a.finish()
    for load in load_factors:
        load.wait()
    pieces_a.begin()
    rows_b.run(0, 3)
    pieces_a.wide()
    pieces_a.run(0, 1)
    rows_b.run(3, 5)
    pieces_a.run(1, 3)
    rows_b.run(5, 8)
    rows_b.finish()
    pieces_b.begin()
    pieces_a.run(3, 8)

    mine_rows = pl.ds(pl.multiple_of(place.chip * PART, PART), PART)
    mine_cols = pl.ds(pl.multiple_of(place.core * SHARE, SHARE), SHARE)

    def swap_to(k):
        to = (r + k) % REP
        return remote(
            inputs.at[mine_rows, columns_of(2 * to + place.core)], parts.at[r, mine_rows, mine_cols], swap_s, swap_r, k, (to, t)
        )

    def swap_from(k):
        source = (r + REP - k) % REP
        ref = parts.at[source, mine_rows, mine_cols]
        return remote(ref, ref, swap_s, swap_r, k, (source, t))

    each(REP, lambda k: swap_to(k).start())
    own_swap = loading(9, inputs.at[mine_rows, columns_of(2 * r + place.core)], parts.at[r, mine_rows, mine_cols])

    def part_view(chunk, low, count):
        at, side = chunk // 2, chunk % 2
        return parts.at[
            pl.ds(low, count),
            pl.ds(pl.multiple_of(at * PART, PART), PART),
            pl.ds(pl.multiple_of(side * SHARE, SHARE), SHARE),
        ]

    ptree = Tree(part_view, place.tp_ids, place.tp_dev, part_s, part_r, REP, REP)
    sibs3 = Siblings(ptree, part_view, REP, place, sib3_s, sib3_r)
    psteps = ptree.steps(sibs3.start)
    gsteps_a = gtree_a.steps(lambda name: None)
    late = []
    gsteps_b = gtree_b.steps(late.append)

    def run(*steps):
        for step in steps:
            step()

    pieces_a.choose()
    gtree_a.begin()
    pieces_b.wide()
    pieces_b.run(0, 3)
    own_swap.wait()
    each(REP, lambda k: swap_from(k).wait_recv())
    ptree.begin()
    sibs3.start("me")
    pieces_b.run(3, 8)
    run(*gsteps_a[:3])
    pieces_b.choose()
    gtree_b.begin()
    own_map.wait()
    each(REP, lambda k: map_from(k).wait_recv())
    load_maps = loading(10, maps_out, maps)
    run(*psteps[:3], *gsteps_a[3:5], *psteps[3:], gsteps_b[0], *gsteps_a[5:], *gsteps_b[1:3])
    for name in ORDER:
        sibs3.wait(name)
    gathered(r, True)
    for step in gsteps_b[3:]:
        while late:
            gathered(gtree_b.names[late.pop(0)])
        step()
    while late:
        gathered(gtree_b.names[late.pop(0)])

    for load in load_state:
        load.wait()

    def strip_of(device):
        return pl.ds(pl.multiple_of(device * STRIP, STRIP), STRIP)

    def one_to(k):
        to = (t + k) % TP
        return remote(strips.at[:, strip_of(to), :], strewn.at[pl.ds(t * SEVEN, SEVEN)], p1_s, p1_r, k, (r, to))

    def adam_rows(n, carry):
        at = pl.ds(pl.multiple_of(n * 16, 16), 16)
        gradient = total[at, :] * SCALING
        first_new = beta_one * one[at, :].astype(F32) + (1.0 - beta_one) * gradient
        second_new = beta_two * two[at, :].astype(F32) + (1.0 - beta_two) * gradient * gradient
        step_size = first_new / bias_one / (jnp.sqrt(second_new / bias_two) + epsilon)
        old = master[at, :]
        new = old - learn_rate * (step_size + weight_decay * old)
        master[at, :] = new
        one[at, :] = first_new.astype(BF16)
        two[at, :] = second_new.astype(BF16)
        low = new.astype(BF16)
        fresh[r, at, :] = low
        for s in range(SEVEN):
            strips[s, at, :] = low[:, s * UNIT : (s + 1) * UNIT]
        return carry

    def strip_done(k, carry):
        to = (t + 1 + k) % TP
        lax.fori_loop(2 * to, 2 * to + 2, adam_rows, 0)

        @pl.when(k < TP - 1)
        def _():
            one_to(k + 1).start()

        return carry

    lax.fori_loop(0, TP, strip_done, 0)

    def fresh_view(chunk, low, count):
        return fresh.at[chunk, pl.ds(low, count), :]

    ftree = Tree(fresh_view, place.rep_ids, place.rep_dev, fresh_s, fresh_r, ROWS, 320)

    def one_from(k):
        source = (t + TP - k) % TP
        ref = strewn.at[pl.ds(source * SEVEN, SEVEN)]
        return remote(ref, ref, p1_s, p1_r, k, (r, source))

    ftree.begin()
    strewn[pl.ds(t * SEVEN, SEVEN)] = strips[:, strip_of(t), :]

    load_maps.wait()
    narrow, rank, count = [], [], jnp.int32(0)
    for q in range(REP):
        narrow.append(maps[q, 0, 0] != -1)
        rank.append(jnp.minimum(count, KINDS - 1))
        count = count + jnp.where(narrow[q], 1, 0)
    which = []
    for k in range(KINDS):
        chosen = jnp.int32(0)
        for q in range(REP):
            chosen = jnp.where(narrow[q] & (rank[q] == k), q, chosen)
        which.append(chosen)

    each(TP, lambda k: one_from(k).wait_recv())
    for k in range(KINDS):

        def pick(to, carry, k=k):
            piece = maps[which[k], 0, to]
            value = strewn[jnp.maximum(piece, 0)]
            picked[to, k] = jnp.where(piece >= 0, value, jnp.zeros_like(value))
            return carry

        lax.fori_loop(0, TP, pick, 0)

    def two_to(k):
        to = (t + k) % TP
        return remote(picked.at[to], routed.at[:, strip_of(t), :], p2_s, p2_r, k, (r, to))

    def two_from(k):
        source = (t + TP - k) % TP
        ref = routed.at[:, strip_of(source), :]
        return remote(ref, ref, p2_s, p2_r, k, (r, source))

    each(TP, lambda k: two_to(k).start())
    routed[:, strip_of(t), :] = picked[t]

    fsteps = ftree.steps(lambda name: None)
    for step in fsteps[:5]:
        step()
    each(TP, lambda k: two_from(k).wait_recv())
    for q in range(REP):
        value = routed[rank[q]]
        outgoing[q] = jnp.where(narrow[q], value, jnp.zeros_like(value))

    def three_to(k):
        to = (r + k) % REP
        return remote(outgoing.at[to], adopted.at[r], p3_s, p3_r, k, (to, t))

    def three_from(k):
        source = (r + REP - k) % REP
        return remote(adopted.at[source], adopted.at[source], p3_s, p3_r, k, (source, t))

    each(REP, lambda k: three_to(k).start())
    adopted[r] = outgoing[r]
    for step in fsteps[5:]:
        step()
    each(REP, lambda k: three_from(k).wait_recv())

    for part in (rows_a, rows_b, pieces_a, pieces_b):
        part.tree.drain()
        part.sibs.drain()
    for book in (ptree, sibs3, gtree_a, gtree_b, ftree):
        book.drain()
    each(REP, lambda k: map_to(k).wait_send())
    each(TP, lambda k: share_to(k).wait_send())
    each(REP, lambda k: swap_to(k).wait_send())
    each(TP, lambda k: one_to(k).wait_send())
    each(TP, lambda k: two_to(k).wait_send())
    each(REP, lambda k: three_to(k).wait_send())


def finish_kernel(
    holders_ref, master, one, two, fresh, adopted, master_out, one_out, two_out, copy_out, stage, outs
):
    failed = holders_ref[0, lax.axis_index("tp")] == -2
    stores = []

    def storing(source, target):
        copy = pltpu.make_async_copy(source, target, outs.at[len(stores)])
        copy.start()
        stores.append(copy)

    storing(master, master_out)
    storing(one, one_out)
    storing(two, two_out)
    for chunk in range(REP):

        def rows(n, carry, chunk=chunk):
            at = pl.ds(pl.multiple_of(n * 32, 32), 32)
            to = pl.ds(pl.multiple_of(chunk * ROWS + n * 32, 32), 32)
            for source, cols in ((fresh, slice(0, WIDE)), (adopted, slice(WIDE, NARROW))):
                value = source[chunk, at, :]
                stage[to, cols] = jnp.where(failed, jnp.zeros_like(value), value)
            return carry

        lax.fori_loop(0, ROWS // 32, rows, 0, unroll=4)
        span = pl.ds(chunk * ROWS, ROWS)
        storing(stage.at[span], copy_out.at[span])
    for store in stores:
        store.wait()


ANY = pl.BlockSpec(memory_space=pl.ANY)
VM = pl.BlockSpec(memory_space=pltpu.VMEM)
SM = pl.BlockSpec(memory_space=pltpu.SMEM)


def sems(*counts):
    return [pltpu.SemaphoreType.DMA((n,)) for n in counts for _ in (0, 1)]


def on_device(
    batch_rows, token_slots, holder_map, copies, upstream, up_act, master, moment1, moment2
):
    state = (
        jax.ShapeDtypeStruct((ROWS, WIDE), F32),
        jax.ShapeDtypeStruct((ROWS, WIDE), BF16),
        jax.ShapeDtypeStruct((ROWS, WIDE), BF16),
    )
    *held, _ = pl.pallas_call(
        step_kernel,
        out_shape=(
            *(pltpu.VMEM(a.shape, a.dtype) for a in state),
            pltpu.VMEM((REP, ROWS, WIDE), BF16),
            pltpu.VMEM((REP, ROWS, UNIT), BF16),
            jax.ShapeDtypeStruct((REP, 1, TP), jnp.int32),
        ),
        in_specs=[ANY, VM, SM, ANY, ANY, ANY, ANY, ANY, ANY, ANY],
        out_specs=(VM, VM, VM, VM, VM, ANY),
        scratch_shapes=[
            pltpu.VMEM((OWN, D), BF16),
            pltpu.VMEM((TP * OWN, SHARE), BF16),
            pltpu.VMEM((TOK, D), BF16),
            pltpu.VMEM((TOK, 128), jnp.int32),
            pltpu.VMEM((TOK, TP * OWN), BF16),
            pltpu.VMEM((D, NARROW), BF16),
            pltpu.VMEM((TOK, NARROW), F32),
            pltpu.VMEM((TOK, NARROW), BF16),
            pltpu.VMEM((TOK, NARROW), BF16),
            pltpu.VMEM((TOK, WIDE), BF16),
            pltpu.VMEM((TP, HALF, UNIT), BF16),
            pltpu.VMEM((TP, HALF, UNIT), BF16),
            pltpu.VMEM((REP, TOK, ROWS), BF16),
            pltpu.VMEM((REP, TOK, WIDE), BF16),
            pltpu.VMEM((ROWS, WIDE), F32),
            pltpu.VMEM((SEVEN, ROWS, UNIT), BF16),
            pltpu.VMEM((TP * SEVEN, STRIP, UNIT), BF16),
            pltpu.VMEM((TP, KINDS, STRIP, UNIT), BF16),
            pltpu.VMEM((KINDS, ROWS, UNIT), BF16),
            pltpu.VMEM((REP, ROWS, UNIT), BF16),
            pltpu.SMEM((REP, 1, TP), jnp.int32),
            *sems(REP, TP, 26, 16, 26, 16),
            *sems(REP, 13, 8, 26, 13, TP, TP, REP),
            pltpu.SemaphoreType.DMA((11,)),
        ],
        compiler_params=pltpu.CompilerParams(
            collective_id=0, has_side_effects=True, vmem_limit_bytes=LIMIT << 20
        ),
        name="step",
    )(
        batch_rows, token_slots, holder_map, holder_map, copies, upstream, up_act,
        master, moment1, moment2,
    )
    return pl.pallas_call(
        finish_kernel,
        out_shape=(*state, jax.ShapeDtypeStruct((D, NARROW), BF16)),
        in_specs=[SM, VM, VM, VM, VM, VM],
        out_specs=(ANY,) * 4,
        scratch_shapes=[pltpu.VMEM((D, NARROW), BF16), pltpu.SemaphoreType.DMA((11,))],
        compiler_params=pltpu.CompilerParams(vmem_limit_bytes=16 << 20),
        name="finish",
    )(holder_map, *held)


def solution(mesh):
    placed = (
        P(("rep", "tp"), None),
        P("rep", None),
        P("rep", None),
        P("rep", "tp"),
        P("rep", "tp"),
        P("rep", "tp"),
        P("rep", "tp"),
        P("rep", "tp"),
        P("rep", "tp"),
    )
    return jax.shard_map(
        on_device,
        mesh=mesh,
        in_specs=placed,
        out_specs=(P("rep", "tp"), P("rep", "tp"), P("rep", "tp"), P("rep", "tp")),
        check_vma=False,
    )
```
